128 devices in a mesh: row: 8 (over y, core), col: 16 (over x, z).
Axes of the slice: x: 4, y: 4, z: 4, core: 2. Of those that a mesh axis runs over, the one named last changes fastest.
Arguments:
- x_feat: bfloat16 [65536, 256], P(('row', 'col')), may hold values from -6 to 6
- block_values: bfloat16 [8, 16, 128, 128, 128], P('row', 'col')
- block_rows: int32 [8, 16, 128], P('row', 'col'), may hold values from 0 to 63, as said below
- block_cols: int32 [8, 16, 128], P('row', 'col'), may hold values from 0 to 31
- weight: bfloat16 [256, 256], replicated, may hold values from -0.375 to 0.375
- bias: float32 [256], replicated, may hold values from -3 to 3
- cotangent: bfloat16 [65536, 256], P(('row', 'col')), may hold values from -6 to 6
Outputs:
- out_act: bfloat16 [65536, 256], P(('row', 'col'))
- x_grad: bfloat16 [65536, 256], P(('row', 'col'))
- weight_grad: float32 [256, 256], replicated
- bias_grad: float32 [256], replicated
The draws below stay inside these ranges and needn't reach their ends.
Inputs may be any that keep to these rules, and one draw needn't show every extreme that they name: `block_rows`: in tile (i, j), slots g * 8 to (g + 1) * 8 - 1 hold blocks of block rows g * 4 to (g + 1) * 4 - 1 of the tile; within a tile no pair of block row and block column repeats.
All inputs are finite; a program needn't handle non-finite values.
Results may differ from the reference program's by a relative error of at most 0.025.
Values may be sent and summed in bfloat16 or wider, within the bound.
No kernel may reach another device: no remote copies, remote signals or barrier semaphores. Data moves between devices by JAX's collectives and lax.ppermute only.
A program may use at most 64 MiB of HBM per device.

```python
import math
import jax
import jax.numpy as jnp
from jax import lax

F = 256
BLK = 128
PB = 4
NNZ_DEV = 128
NODES = 65536
N_ROW = 8
N_COL = 16


def choose_slots(group_key):
    return jax.random.permutation(group_key, PB * N_ROW * PB)[:NNZ_DEV // N_COL]


def block_layout(key):
    group_total = N_ROW * N_COL * N_COL
    group_keys = jax.random.split(jax.random.fold_in(key, 11), group_total)
    slots = jax.vmap(choose_slots)(group_keys).astype(jnp.int32)
    slots = slots.reshape(N_ROW, N_COL, N_COL, NNZ_DEV // N_COL)
    group_index = jnp.arange(N_COL, dtype=jnp.int32)[None, None, :, None]
    rows_out = group_index * PB + slots // (N_ROW * PB)
    cols_out = slots % (N_ROW * PB)
    return (rows_out.reshape(N_ROW, N_COL, NNZ_DEV).astype(jnp.int32), cols_out.reshape(N_ROW, N_COL, NNZ_DEV).astype(jnp.int32))


def draw_block_rows(key, part):
    return block_layout(key)[0]


def draw_block_cols(key, part):
    return block_layout(key)[1]


def draw_block_values(key, part):
    shape = (N_ROW, N_COL, NNZ_DEV, BLK, BLK)
    candidates = NNZ_DEV * BLK / PB
    density = min(1.0, 40.0 * PB / (NNZ_DEV * BLK))
    expected = candidates * density
    mask_key = jax.random.fold_in(key, 23)
    value_key = jax.random.fold_in(key, 29)
    present = jax.random.bernoulli(mask_key, density, shape).astype(jnp.float32)
    entries = jax.random.normal(value_key, shape, jnp.float32)
    return (present * entries / expected ** 0.5).astype(jnp.bfloat16)


def shard_levels(own_key, shape, cuts, low, top_value):
    def one(dim, shards_of):
        steps = jax.random.uniform(jax.random.fold_in(jax.random.fold_in(own_key, 6), dim), (shards_of,), jnp.float32, low / len(cuts), top_value / len(cuts))
        return jnp.repeat(jnp.exp(steps), shape[dim] // shards_of).reshape((-1,) + (1,) * (len(shape) - dim - 1))

    loudness = one(*cuts[0])
    for cut in cuts[1:]:
        loudness = loudness * one(*cut)
    return loudness


def centred(stream_key, shape, width, reach, cuts=(), kind=jnp.bfloat16):
    gain = shard_levels(stream_key, shape, cuts, -0.22, 0.18) if cuts else 1.0
    values = jax.random.normal(stream_key, shape, jnp.float32) * width * gain
    return jnp.minimum(jnp.maximum(values, -reach), reach).astype(kind)


def setup_inputs(seed: int = 0) -> dict:
    key_list = jax.random.split(jax.random.key(seed), 8)
    return {
        "x_feat": centred(key_list[0], (NODES, F), 1.0, 6.0, ((0, 128),)),
        "block_values": draw_block_values(jax.random.fold_in(key_list[7], 71), 0),
        "block_rows": draw_block_rows(jax.random.fold_in(key_list[7], 71), 0),
        "block_cols": draw_block_cols(jax.random.fold_in(key_list[7], 71), 0),
        "weight": centred(key_list[4], (F, F), F ** -0.5, 0.375),
        "bias": centred(key_list[5], (F,), 0.5, 3.0, (), jnp.float32),
        "cotangent": centred(key_list[6], (NODES, F), 1.0, 6.0, ((0, 128),)),
    }


def reference(x_feat, block_values, block_rows, block_cols, weight, bias, cotangent):
    shard_rows = PB * BLK
    x_four = x_feat.reshape(N_ROW, N_COL, shard_rows, F)

    def forward_tile(accum, tile):
        row_idx = tile // N_COL
        col_idx = tile % N_COL
        tile_values = block_values[row_idx, col_idx].astype(jnp.float32)
        panel_blocks = x_four[:, col_idx].reshape(N_ROW * PB, BLK, F).astype(jnp.float32)
        picked = panel_blocks[block_cols[row_idx, col_idx]]
        products = jnp.einsum('bij,bjf->bif', tile_values, picked, precision=lax.Precision.HIGHEST)
        partial_sum = jnp.zeros((N_COL * PB, BLK, F), jnp.float32).at[block_rows[row_idx, col_idx]].add(products)
        rounded = lax.optimization_barrier(partial_sum.astype(jnp.bfloat16)).astype(jnp.float32)
        accum = accum.at[row_idx].add(rounded.reshape(N_COL, shard_rows, F))
        return (accum, None)
    forward_sum, _ = lax.scan(forward_tile, jnp.zeros((N_ROW, N_COL, shard_rows, F), jnp.float32), jnp.arange(N_ROW * N_COL, dtype=jnp.int32))
    aggregated = forward_sum.reshape(NODES, F).astype(jnp.bfloat16)
    pre = jnp.dot(aggregated, weight, preferred_element_type=jnp.float32) + bias
    sigmoid_pre = jax.nn.sigmoid(pre)
    out_act = (pre * sigmoid_pre).astype(jnp.bfloat16)
    grad_pre = (cotangent.astype(jnp.float32) * sigmoid_pre * (1.0 + pre * (1.0 - sigmoid_pre))).astype(jnp.bfloat16)
    scale = 1.0 / math.sqrt(NODES)
    weight_grad = jnp.dot(aggregated.T, grad_pre, preferred_element_type=jnp.float32) * scale
    bias_grad = lax.optimization_barrier(jnp.sum(grad_pre.astype(jnp.float32), axis=0)) * scale
    grad_agg = jnp.dot(grad_pre, weight.T, preferred_element_type=jnp.float32).astype(jnp.bfloat16)
    grad_four = grad_agg.reshape(N_ROW, N_COL, shard_rows, F)

    def backward_tile(accum, tile):
        row_idx = tile // N_COL
        col_idx = tile % N_COL
        tile_values = block_values[row_idx, col_idx].astype(jnp.float32)
        grad_blocks = grad_four[row_idx].reshape(N_COL * PB, BLK, F).astype(jnp.float32)
        picked = grad_blocks[block_rows[row_idx, col_idx]]
        products = jnp.einsum('bij,bif->bjf', tile_values, picked, precision=lax.Precision.HIGHEST)
        partial_sum = jnp.zeros((N_ROW * PB, BLK, F), jnp.float32).at[block_cols[row_idx, col_idx]].add(products)
        rounded = lax.optimization_barrier(partial_sum.astype(jnp.bfloat16)).astype(jnp.float32)
        accum = accum.at[:, col_idx].add(rounded.reshape(N_ROW, shard_rows, F))
        return (accum, None)
    backward_sum, _ = lax.scan(backward_tile, jnp.zeros((N_ROW, N_COL, shard_rows, F), jnp.float32), jnp.arange(N_ROW * N_COL, dtype=jnp.int32))
    x_grad = backward_sum.reshape(NODES, F).astype(jnp.bfloat16)
    return (out_act, x_grad, weight_grad, bias_grad)
```

```python
import math

import jax
import jax.numpy as jnp
from jax import lax
from jax.experimental import pallas as pl
from jax.experimental.pallas import tpu as pltpu
from jax.sharding import PartitionSpec as P

BF = jnp.bfloat16
F32 = jnp.float32
BLK = 128
PB = 4
ROWS = 512
HALF = 128
F = 256
GRP = 8
MIB = 1 << 20


def vmem():
    return pl.BlockSpec(memory_space=pltpu.VMEM)


def smem():
    return pl.BlockSpec(memory_space=pltpu.SMEM)


def hbm():
    return pl.BlockSpec(memory_space=pl.ANY)


def coords():
    row = lax.axis_index("row")
    col = lax.axis_index("col")
    return col // 4, col % 4, row // 2, row % 2


def fetch_values(values, held, sems, group, step):
    copy = pltpu.make_async_copy(
        values.at[pl.ds(group * GRP, GRP)], held.at[step], sems.at[step]
    )
    return copy


def forward_kernel(rows, cols, values, *refs):
    pieces = refs[:8]
    outs_a = refs[8:12]
    outs_b = refs[12:16]
    panel, held, acc, piece_sems, value_sems = refs[16:]
    x, z, y, c = coords()

    def piece_copy(n):
        dy, dc = n % 4, n // 4
        shard = ((y + 4 - dy) % 4) * 2 + (c + dc) % 2
        return pltpu.make_async_copy(
            pieces[n], panel.at[pl.ds(shard * ROWS, ROWS)], piece_sems.at[n]
        )

    def group_of(step):
        p, r = step // 4, step % 4
        return ((x + p) % 4) * 4 + (z + r) % 4

    for n in range(8):
        piece_copy(n).start()
    for step in range(16):
        fetch_values(values, held, value_sems, group_of(step), step).start()
    for n in range(8):
        piece_copy(n).wait()
    for step in range(16):
        p, r = step // 4, step % 4
        group = group_of(step)
        fetch_values(values, held, value_sems, group, step).wait()
        acc[...] = jnp.zeros_like(acc)
        for k in range(GRP):
            local = rows[0, group * GRP + k] - group * PB
            block = cols[0, group * GRP + k]
            here = pl.ds(pl.multiple_of(local * BLK, BLK), BLK)
            there = pl.ds(pl.multiple_of(block * BLK, BLK), BLK)
            acc[here, :] += jnp.dot(
                held[step, k], panel[there, :], preferred_element_type=F32
            )
        outs_a[p][r * ROWS:(r + 1) * ROWS, :] = acc[:, :HALF].astype(BF)
        outs_b[r][p * ROWS:(p + 1) * ROWS, :] = acc[:, HALF:].astype(BF)


def forward_call(rows, cols, values, pieces):
    part = jax.ShapeDtypeStruct((4 * ROWS, HALF), BF)
    return pl.pallas_call(
        forward_kernel,
        out_shape=[part] * 8,
        in_specs=[smem(), smem(), hbm()] + [hbm()] * 8,
        out_specs=[vmem()] * 8,
        scratch_shapes=[
            pltpu.VMEM((8 * ROWS, F), BF),
            pltpu.VMEM((16, GRP, BLK, BLK), BF),
            pltpu.VMEM((ROWS, F), F32),
            pltpu.SemaphoreType.DMA((8,)),
            pltpu.SemaphoreType.DMA((16,)),
        ],
        compiler_params=pltpu.CompilerParams(vmem_limit_bytes=40 * MIB),
        cost_estimate=pl.CostEstimate(
            flops=2 * 128 * BLK * BLK * F, bytes_accessed=10 * MIB, transcendentals=0
        ),
        name="forward_tile",
    )(rows, cols, values, *pieces)


def add_kernel(*refs):
    total = (refs[0][...].astype(F32) + refs[2][...].astype(F32)) + (
        refs[1][...].astype(F32) + refs[3][...].astype(F32)
    )
    total = total.astype(BF)
    for n, out in enumerate(refs[4:]):
        out[...] = total[n * ROWS:(n + 1) * ROWS, :]


def add_call(parts, width, count, name):
    out = jax.ShapeDtypeStruct((ROWS, width), BF)
    return pl.pallas_call(
        add_kernel,
        out_shape=[out] * count,
        in_specs=[vmem()] * 4,
        out_specs=[vmem()] * count,
        compiler_params=pltpu.CompilerParams(vmem_limit_bytes=24 * MIB),
        cost_estimate=pl.CostEstimate(
            flops=4 * count * ROWS * width, bytes_accessed=10 * count * ROWS * width,
            transcendentals=0,
        ),
        name=name,
    )(*parts)


def point_kernel(scale, *refs):
    parts_a = refs[:4]
    parts_b = refs[4:8]
    weight, bias, cotangent = refs[8:11]
    out_act, grad_a, grad_b, gradients = refs[11:]

    def join(parts):
        return (
            (parts[0][...].astype(F32) + parts[2][...].astype(F32))
            + (parts[1][...].astype(F32) + parts[3][...].astype(F32))
        ).astype(BF)

    aggregated = jnp.concatenate([join(parts_a), join(parts_b)], axis=1)
    pre = jnp.dot(aggregated, weight[...], preferred_element_type=F32) + bias[...]
    gate = jax.nn.sigmoid(pre)
    out_act[...] = (pre * gate).astype(BF)
    grad_pre = (
        cotangent[...].astype(F32) * gate * (1.0 + pre * (1.0 - gate))
    ).astype(BF)
    grad_agg = lax.dot_general(
        grad_pre, weight[...], (((1,), (1,)), ((), ())), preferred_element_type=F32
    ).astype(BF)
    grad_a[...] = grad_agg[:, :HALF]
    grad_b[...] = grad_agg[:, HALF:]
    weight_grad = lax.dot_general(
        aggregated, grad_pre, (((0,), (0,)), ((), ())), preferred_element_type=F32
    ) * scale
    bias_grad = jnp.sum(grad_pre.astype(F32), axis=0, keepdims=True) * scale
    for n in range(8):
        gradients[n, :32, :] = weight_grad[n * 32:(n + 1) * 32, :]
        gradients[n, 32:, :] = jnp.broadcast_to(bias_grad, (8, F))


def point_call(parts_a, parts_b, weight, bias, cotangent, scale):
    half = jax.ShapeDtypeStruct((ROWS, HALF), BF)
    return pl.pallas_call(
        lambda *refs: point_kernel(scale, *refs),
        out_shape=[
            jax.ShapeDtypeStruct((ROWS, F), BF),
            half,
            half,
            jax.ShapeDtypeStruct((8, 40, F), F32),
        ],
        in_specs=[vmem()] * 11,
        out_specs=[vmem()] * 4,
        compiler_params=pltpu.CompilerParams(vmem_limit_bytes=24 * MIB),
        cost_estimate=pl.CostEstimate(
            flops=3 * 2 * ROWS * F * F, bytes_accessed=2 * MIB, transcendentals=ROWS * F
        ),
        name="pointwise",
    )(*parts_a, *parts_b, weight, bias, cotangent)


def backward_kernel(rows, cols, values, *refs):
    parts_a = refs[:4]
    parts_b = refs[4:8]
    mine, other = refs[8:10]
    acc, held, value_sems = refs[10:]
    x, z, y, c = coords()

    def group_of(step):
        p, r = step // 4, step % 4
        return ((x + 4 - p) % 4) * 4 + (z + 4 - r) % 4

    for step in range(16):
        fetch_values(values, held, value_sems, group_of(step), step).start()
    acc[...] = jnp.zeros_like(acc)
    for step in range(16):
        p, r = step // 4, step % 4
        group = group_of(step)
        fetch_values(values, held, value_sems, group, step).wait()
        for k in range(GRP):
            local = rows[0, group * GRP + k] - group * PB
            block = cols[0, group * GRP + k]
            in_a = pl.ds(pl.multiple_of(r * ROWS + local * BLK, BLK), BLK)
            in_b = pl.ds(pl.multiple_of(p * ROWS + local * BLK, BLK), BLK)
            grads = jnp.concatenate([parts_a[p][in_a, :], parts_b[r][in_b, :]], axis=1)
            there = pl.ds(pl.multiple_of(block * BLK, BLK), BLK)
            acc[there, :] += lax.dot_general(
                held[step, k], grads, (((0,), (0,)), ((), ())), preferred_element_type=F32
            )
    for dy in range(4):
        base = ((y + dy) % 4) * 2
        own = pl.ds(pl.multiple_of((base + c) * ROWS, ROWS), ROWS)
        peer = pl.ds(pl.multiple_of((base + 1 - c) * ROWS, ROWS), ROWS)
        mine[dy * ROWS:(dy + 1) * ROWS, :] = acc[own, :].astype(BF)
        other[dy * ROWS:(dy + 1) * ROWS, :] = acc[peer, :].astype(BF)


def backward_call(rows, cols, values, parts_a, parts_b):
    part = jax.ShapeDtypeStruct((4 * ROWS, F), BF)
    return pl.pallas_call(
        backward_kernel,
        out_shape=[part] * 2,
        in_specs=[smem(), smem(), hbm()] + [vmem()] * 8,
        out_specs=[vmem()] * 2,
        scratch_shapes=[
            pltpu.VMEM((8 * ROWS, F), F32),
            pltpu.VMEM((16, GRP, BLK, BLK), BF),
            pltpu.SemaphoreType.DMA((16,)),
        ],
        compiler_params=pltpu.CompilerParams(vmem_limit_bytes=40 * MIB),
        cost_estimate=pl.CostEstimate(
            flops=2 * 128 * BLK * BLK * F, bytes_accessed=10 * MIB, transcendentals=0
        ),
        name="backward_tile",
    )(rows, cols, values, *parts_a, *parts_b)


def pair_kernel(mine, other, *outs):
    for n, out in enumerate(outs):
        here = pl.ds(n * ROWS, ROWS)
        out[...] = (mine[here, :].astype(F32) + other[here, :].astype(F32)).astype(BF)


def pair_call(mine, other):
    out = jax.ShapeDtypeStruct((ROWS, F), BF)
    return pl.pallas_call(
        pair_kernel,
        out_shape=[out] * 4,
        in_specs=[vmem()] * 2,
        out_specs=[vmem()] * 4,
        compiler_params=pltpu.CompilerParams(vmem_limit_bytes=24 * MIB),
        cost_estimate=pl.CostEstimate(
            flops=4 * ROWS * F, bytes_accessed=24 * ROWS * F, transcendentals=0
        ),
        name="pair_sum",
    )(mine, other)


def along_col(value, dx, dz):
    pairs = [
        (a * 4 + b, ((a + dx) % 4) * 4 + (b + dz) % 4) for a in range(4) for b in range(4)
    ]
    return lax.ppermute(value, "col", pairs)


def along_row(value, dy, dc):
    pairs = [
        (a * 2 + b, ((a + dy) % 4) * 2 + (b + dc) % 2) for a in range(4) for b in range(2)
    ]
    return lax.ppermute(value, "row", pairs)


def shards(x_feat, block_values, block_rows, block_cols, weight, bias, cotangent):
    values = block_values.reshape(128, BLK, BLK)
    rows = block_rows.reshape(1, 128)
    cols = block_cols.reshape(1, 128)
    scale = 1.0 / math.sqrt(65536)

    near = {d: along_row(x_feat, d, 0) for d in (2, 1, 3)}
    swap = [along_row(x_feat, 0, 1)] + [None] * 3
    for d in (1, 3, 2):
        swap[d] = along_row(near[d], 0, 1)
    pieces = [x_feat, near[1], near[2], near[3]] + swap

    outs = forward_call(rows, cols, values, pieces)
    outs_a, outs_b = outs[:4], outs[4:]
    got_a, got_b = [outs_a[0]] + [None] * 3, [outs_b[0]] + [None] * 3
    for d in (2, 1, 3):
        got_a[d] = along_col(outs_a[d], d, 0)
        got_b[d] = along_col(outs_b[d], 0, d)
    sum_a = add_call(got_a, HALF, 4, "sum_a")
    sum_b = add_call(got_b, HALF, 4, "sum_b")
    part_a, part_b = [sum_a[0]] + [None] * 3, [sum_b[0]] + [None] * 3
    for d in (2, 1, 3):
        part_a[d] = along_col(sum_a[d], 0, d)
        part_b[d] = along_col(sum_b[d], d, 0)
    out_act, grad_a, grad_b, gradients = point_call(
        part_a, part_b, weight, bias.reshape(1, F), cotangent, scale
    )

    first_a, first_b = [grad_a] + [None] * 3, [grad_b] + [None] * 3
    for d in (2, 1, 3):
        first_a[d] = along_col(grad_a, 0, d)
        first_b[d] = along_col(grad_b, d, 0)
    join_a = jnp.concatenate(first_a, axis=0)
    join_b = jnp.concatenate(first_b, axis=0)
    full_a, full_b = [join_a] + [None] * 3, [join_b] + [None] * 3
    for d in (2, 1, 3):
        full_a[d] = along_col(join_a, d, 0)
        full_b[d] = along_col(join_b, 0, d)

    spread = lax.all_to_all(gradients, "row", 0, 0)
    piece = jnp.sum(spread, axis=0)
    for dx, dz in ((1, 0), (0, 1)):
        r1, r2, r3 = (along_col(piece, d * dx, d * dz) for d in (1, 2, 3))
        piece = (piece + r2) + (r1 + r3)
    complete = lax.all_gather(piece, "row", axis=0, tiled=False)
    weight_grad = complete[:, :32, :].reshape(F, F)
    bias_grad = complete[0, 32, :]

    mine, other = backward_call(rows, cols, values, full_a, full_b)
    other = along_row(other, 0, 1)
    sums = pair_call(mine, other)
    last = [sums[0]] + [None] * 3
    for d in (2, 1, 3):
        last[d] = along_row(sums[d], d, 0)
    x_grad = add_call(last, F, 1, "sum_x")[0]
    return (out_act, x_grad, weight_grad, bias_grad)


def solution(mesh):
    placed = (
        P(("row", "col"), None),
        P("row", "col", None, None, None),
        P("row", "col", None),
        P("row", "col", None),
        P(),
        P(),
        P(("row", "col"), None),
    )
    return jax.shard_map(
        shards,
        mesh=mesh,
        in_specs=placed,
        out_specs=(P(("row", "col"), None), P(("row", "col"), None), P(), P()),
        check_vma=False,
    )
```

```python
import math

import jax
import jax.numpy as jnp
from jax import lax
from jax.experimental import pallas as pl
from jax.experimental.pallas import tpu as pltpu
from jax.sharding import PartitionSpec as P

BF = jnp.bfloat16
F32 = jnp.float32
BLK = 128
PB = 4
ROWS = 512
HALF = 128
F = 256
GRP = 8
MIB = 1 << 20


def vmem():
    return pl.BlockSpec(memory_space=pltpu.VMEM)


def smem():
    return pl.BlockSpec(memory_space=pltpu.SMEM)


def hbm():
    return pl.BlockSpec(memory_space=pl.ANY)


def coords():
    row = lax.axis_index("row")
    col = lax.axis_index("col")
    return col // 4, col % 4, row // 2, row % 2


def prologue_kernel(*refs):
    count = (len(refs) - 1) // 2
    sems = refs[-1]
    copies = [
        pltpu.make_async_copy(refs[n], refs[count + n], sems.at[n]) for n in range(count)
    ]
    for copy in copies:
        copy.start()
    for copy in copies:
        copy.wait()


def prologue_call(arrays):
    return pl.pallas_call(
        prologue_kernel,
        out_shape=[jax.ShapeDtypeStruct(a.shape, a.dtype) for a in arrays],
        in_specs=[pl.BlockSpec(memory_space=pltpu.HBM)] * len(arrays),
        out_specs=[vmem()] * len(arrays),
        scratch_shapes=[pltpu.SemaphoreType.DMA((len(arrays),))],
        compiler_params=pltpu.CompilerParams(vmem_limit_bytes=8 * MIB),
        cost_estimate=pl.CostEstimate(
            flops=0, bytes_accessed=10 * MIB, transcendentals=0
        ),
        name="prologue",
    )(*arrays)


def forward_group(rows, cols, values, panel, acc, group, lanes):
    acc[:, lanes] = jnp.zeros_like(acc[:, lanes])
    for k in range(GRP):
        local = rows[0, group * GRP + k] - group * PB
        block = cols[0, group * GRP + k]
        here = pl.ds(pl.multiple_of(local * BLK, BLK), BLK)
        there = pl.ds(pl.multiple_of(block * BLK, BLK), BLK)
        acc[here, lanes] += jnp.dot(
            values[group * GRP + k], panel[there, lanes], preferred_element_type=F32
        )


def target_group(x, z, p, r):
    return ((x + p) % 4) * 4 + (z + r) % 4


LOW, HIGH, ALL = slice(0, HALF), slice(HALF, F), slice(0, F)


def far_kernel(rows, cols, values, *refs):
    pieces = refs[:8]
    panel = refs[8]
    outs_a = refs[9:11]
    outs_b = refs[11:13]
    acc, sems = refs[13:]
    x, z, y, c = coords()
    copies = []
    for n in range(8):
        dy, dc = n % 4, n // 4
        shard = ((y + 4 - dy) % 4) * 2 + (c + dc) % 2
        copies.append(
            pltpu.make_async_copy(
                pieces[n], panel.at[pl.ds(shard * ROWS, ROWS)], sems.at[n]
            )
        )
    for copy in copies:
        copy.start()
    for copy in copies:
        copy.wait()
    for n in range(4):
        lanes = ALL if n == 2 else LOW
        forward_group(rows, cols, values, panel, acc, target_group(x, z, 2, n), lanes)
        here = pl.ds((n % 2) * ROWS, ROWS)
        outs_a[n // 2][here, :] = acc[:, LOW].astype(BF)
        if n == 2:
            outs_b[n // 2][here, :] = acc[:, HIGH].astype(BF)
    for n in (0, 1, 3):
        forward_group(rows, cols, values, panel, acc, target_group(x, z, n, 2), HIGH)
        here = pl.ds((n % 2) * ROWS, ROWS)
        outs_b[n // 2][here, :] = acc[:, HIGH].astype(BF)


def far_call(rows, cols, values, pieces):
    part = jax.ShapeDtypeStruct((2 * ROWS, HALF), BF)
    return pl.pallas_call(
        far_kernel,
        out_shape=[jax.ShapeDtypeStruct((8 * ROWS, F), BF)] + [part] * 4,
        in_specs=[smem(), smem(), vmem()] + [hbm()] * 8,
        out_specs=[vmem()] * 5,
        scratch_shapes=[pltpu.VMEM((ROWS, F), F32), pltpu.SemaphoreType.DMA((8,))],
        compiler_params=pltpu.CompilerParams(vmem_limit_bytes=24 * MIB),
        cost_estimate=pl.CostEstimate(
            flops=32 * 2 * BLK * BLK * F, bytes_accessed=7 * MIB, transcendentals=0
        ),
        name="forward_far",
    )(rows, cols, values, *pieces)


def near_kernel(rows, cols, values, panel, *refs):
    outs_a = (refs[0], refs[1], None, refs[2])
    outs_b = (refs[3], refs[4], None, refs[5])
    acc = refs[6]
    x, z, y, c = coords()
    for p in (1, 3, 0, 2):
        for r in (1, 3, 0, 2):
            if p == 2 and r == 2:
                continue
            lanes = HIGH if p == 2 else LOW if r == 2 else ALL
            forward_group(rows, cols, values, panel, acc, target_group(x, z, p, r), lanes)
            if p != 2:
                outs_a[p][r * ROWS:(r + 1) * ROWS, :] = acc[:, LOW].astype(BF)
            if r != 2:
                outs_b[r][p * ROWS:(p + 1) * ROWS, :] = acc[:, HIGH].astype(BF)


def near_call(rows, cols, values, panel):
    part = jax.ShapeDtypeStruct((4 * ROWS, HALF), BF)
    return pl.pallas_call(
        near_kernel,
        out_shape=[part] * 6,
        in_specs=[smem(), smem(), vmem(), vmem()],
        out_specs=[vmem()] * 6,
        scratch_shapes=[pltpu.VMEM((ROWS, F), F32)],
        compiler_params=pltpu.CompilerParams(vmem_limit_bytes=24 * MIB),
        cost_estimate=pl.CostEstimate(
            flops=96 * 2 * BLK * BLK * F, bytes_accessed=9 * MIB, transcendentals=0
        ),
        name="forward_near",
    )(rows, cols, values, panel)


def relay_kernel(*refs):
    for n in range(4):
        own, extra, out = refs[n], refs[4 + n], refs[8 + n]
        mixed = pl.ds((n % 2) * 2 * ROWS, 2 * ROWS)
        plain = pl.ds((1 - n % 2) * 2 * ROWS, 2 * ROWS)
        out[mixed, :] = (own[mixed, :].astype(F32) + extra[...].astype(F32)).astype(BF)
        out[plain, :] = own[plain, :]


def relay_call(own, extra):
    return pl.pallas_call(
        relay_kernel,
        out_shape=[jax.ShapeDtypeStruct((4 * ROWS, HALF), BF)] * 4,
        in_specs=[vmem()] * 8,
        out_specs=[vmem()] * 4,
        compiler_params=pltpu.CompilerParams(vmem_limit_bytes=24 * MIB),
        cost_estimate=pl.CostEstimate(
            flops=8 * ROWS * HALF, bytes_accessed=5 * MIB, transcendentals=0
        ),
        name="relay_sum",
    )(*own, *extra)


def quad(parts, here=slice(None)):
    p0, p1, p2, p3 = (part[here].astype(F32) for part in parts)
    return (p0 + p2) + (p1 + p3)


def stage_kernel(*refs):
    for half in range(2):
        parts = refs[3 * half:3 * half + 3]
        outs = refs[6 + 4 * half:10 + 4 * half]
        for n, out in enumerate(outs):
            here = pl.ds(n * ROWS, ROWS)
            p0, p1, p3 = (part[here, :].astype(F32) for part in parts)
            out[...] = (p0 + (p1 + p3)).astype(BF)


def stage_call(parts_a, parts_b):
    return pl.pallas_call(
        stage_kernel,
        out_shape=[jax.ShapeDtypeStruct((ROWS, HALF), BF)] * 8,
        in_specs=[vmem()] * 6,
        out_specs=[vmem()] * 8,
        compiler_params=pltpu.CompilerParams(vmem_limit_bytes=24 * MIB),
        cost_estimate=pl.CostEstimate(
            flops=24 * ROWS * HALF, bytes_accessed=4 * MIB, transcendentals=0
        ),
        name="stage_sum",
    )(*parts_a, *parts_b)


def point_kernel(scale, *refs):
    parts_a = refs[:4]
    parts_b = refs[4:8]
    weight, bias, cotangent = refs[8:11]
    out_act, grad_a, grad_b, gradients = refs[11:]

    aggregated = jnp.concatenate(
        [quad(parts_a).astype(BF), quad(parts_b).astype(BF)], axis=1
    )
    pre = jnp.dot(aggregated, weight[...], preferred_element_type=F32) + bias[...]
    gate = jax.nn.sigmoid(pre)
    out_act[...] = (pre * gate).astype(BF)
    grad_pre = (
        cotangent[...].astype(F32) * gate * (1.0 + pre * (1.0 - gate))
    ).astype(BF)
    grad_agg = lax.dot_general(
        grad_pre, weight[...], (((1,), (1,)), ((), ())), preferred_element_type=F32
    ).astype(BF)
    grad_a[...] = grad_agg[:, :HALF]
    grad_b[...] = grad_agg[:, HALF:]
    weight_grad = lax.dot_general(
        aggregated, grad_pre, (((0,), (0,)), ((), ())), preferred_element_type=F32
    ) * scale
    bias_grad = jnp.sum(grad_pre.astype(F32), axis=0, keepdims=True) * scale
    for n in range(8):
        gradients[n, :32, :] = weight_grad[n * 32:(n + 1) * 32, :]
        gradients[n, 32:, :] = jnp.broadcast_to(bias_grad, (8, F))


def point_call(parts_a, parts_b, weight, bias, cotangent, scale):
    half = jax.ShapeDtypeStruct((ROWS, HALF), BF)
    return pl.pallas_call(
        lambda *refs: point_kernel(scale, *refs),
        out_shape=[
            jax.ShapeDtypeStruct((ROWS, F), BF),
            half,
            half,
            jax.ShapeDtypeStruct((8, 40, F), F32),
        ],
        in_specs=[vmem()] * 11,
        out_specs=[vmem()] * 4,
        compiler_params=pltpu.CompilerParams(vmem_limit_bytes=24 * MIB),
        cost_estimate=pl.CostEstimate(
            flops=3 * 2 * ROWS * F * F, bytes_accessed=2 * MIB, transcendentals=ROWS * F
        ),
        name="pointwise",
    )(*parts_a, *parts_b, weight, bias, cotangent)


def join_kernel(*refs):
    spread = refs[8]
    outs = refs[9:11]
    for half in range(2):
        for n in range(4):
            outs[half][n * ROWS:(n + 1) * ROWS, :] = refs[4 * half + n][...]
    refs[11][...] = jnp.sum(spread[...], axis=0)


def join_call(parts_a, parts_b, spread):
    return pl.pallas_call(
        join_kernel,
        out_shape=[jax.ShapeDtypeStruct((4 * ROWS, HALF), BF)] * 2
        + [jax.ShapeDtypeStruct((40, F), F32)],
        in_specs=[vmem()] * 9,
        out_specs=[vmem()] * 3,
        compiler_params=pltpu.CompilerParams(vmem_limit_bytes=24 * MIB),
        cost_estimate=pl.CostEstimate(
            flops=320 * F, bytes_accessed=3 * MIB, transcendentals=0
        ),
        name="join",
    )(*parts_a, *parts_b, spread)


def cut_kernel(*refs):
    for n in range(4):
        refs[4 + n][...] = refs[n][pl.ds((n % 2) * 2 * ROWS, 2 * ROWS), :]


def cut_call(parts):
    return pl.pallas_call(
        cut_kernel,
        out_shape=[jax.ShapeDtypeStruct((2 * ROWS, HALF), BF)] * 4,
        in_specs=[vmem()] * 4,
        out_specs=[vmem()] * 4,
        compiler_params=pltpu.CompilerParams(vmem_limit_bytes=16 * MIB),
        cost_estimate=pl.CostEstimate(
            flops=0, bytes_accessed=2 * MIB, transcendentals=0
        ),
        name="cut",
    )(*parts)


def last_kernel(*refs):
    mine, theirs, x_grad, weight_grad, bias_grad = refs[4:]
    x, z, y, c = coords()
    x_grad[...] = quad(refs[:4]).astype(BF)
    for dy in range(4):
        base = ((y + 4 - dy) % 4) * 2
        for source, core in ((mine, c), (theirs, 1 - c)):
            shard = base + core
            here = pl.ds(pl.multiple_of(shard * 32, 32), 32)
            weight_grad[here, :] = source[dy, :32, :]

            @pl.when(shard == 0)
            def _():
                bias_grad[...] = source[dy, 32:33, :]


def last_call(parts, mine, theirs):
    return pl.pallas_call(
        last_kernel,
        out_shape=[
            jax.ShapeDtypeStruct((ROWS, F), BF),
            jax.ShapeDtypeStruct((F, F), F32),
            jax.ShapeDtypeStruct((1, F), F32),
        ],
        in_specs=[vmem()] * 6,
        out_specs=[vmem()] * 3,
        compiler_params=pltpu.CompilerParams(vmem_limit_bytes=24 * MIB),
        cost_estimate=pl.CostEstimate(
            flops=4 * ROWS * F, bytes_accessed=10 * ROWS * F, transcendentals=0
        ),
        name="last_sum",
    )(*parts, mine, theirs)


def backward_slots(rows, cols, values, acc, group, lanes, read):
    for k in range(GRP):
        local = rows[0, group * GRP + k] - group * PB
        there = pl.ds(pl.multiple_of(cols[0, group * GRP + k] * BLK, BLK), BLK)
        acc[there, lanes] += lax.dot_general(
            values[group * GRP + k],
            read(local),
            (((0,), (0,)), ((), ())),
            preferred_element_type=F32,
        )


def source_group(x, z, p, r):
    return ((x + 4 - p) % 4) * 4 + (z + 4 - r) % 4


def block_at(base, local):
    return pl.ds(pl.multiple_of(base + local * BLK, BLK), BLK)


def early_kernel(rows, cols, values, *refs):
    parts_a = (refs[0], refs[1], None, refs[2])
    parts_b = (refs[3], refs[4], None, refs[5])
    acc = refs[6]
    x, z, y, c = coords()
    acc[...] = jnp.zeros_like(acc)
    for p in range(4):
        for r in range(4):
            if p == 2 and r == 2:
                continue

            def from_a(local, p=p, r=r):
                return parts_a[p][block_at(r * ROWS, local), :]

            def from_b(local, p=p, r=r):
                return parts_b[r][block_at(p * ROWS, local), :]

            def both(local, from_a=from_a, from_b=from_b):
                return jnp.concatenate([from_a(local), from_b(local)], axis=1)

            lanes, read = (HIGH, from_b) if p == 2 else (LOW, from_a) if r == 2 else (ALL, both)
            backward_slots(rows, cols, values, acc, source_group(x, z, p, r), lanes, read)


def early_call(rows, cols, values, parts_a, parts_b):
    return pl.pallas_call(
        early_kernel,
        out_shape=jax.ShapeDtypeStruct((8 * ROWS, F), F32),
        in_specs=[smem(), smem()] + [vmem()] * 7,
        out_specs=vmem(),
        compiler_params=pltpu.CompilerParams(vmem_limit_bytes=24 * MIB),
        cost_estimate=pl.CostEstimate(
            flops=96 * 2 * BLK * BLK * F, bytes_accessed=10 * MIB, transcendentals=0
        ),
        name="backward_early",
    )(rows, cols, values, *parts_a, *parts_b)


def late_kernel(rows, cols, values, start, *refs):
    parts_a = refs[:2]
    parts_b = refs[2:4]
    mine, other, acc = refs[4:]
    x, z, y, c = coords()
    acc[...] = start[...]
    for n in range(4):

        def from_a(local, n=n):
            return parts_a[n // 2][block_at((n % 2) * ROWS, local), :]

        def from_b(local, n=n):
            return parts_b[n // 2][block_at((n % 2) * ROWS, local), :]

        backward_slots(rows, cols, values, acc, source_group(x, z, 2, n), LOW, from_a)
        backward_slots(rows, cols, values, acc, source_group(x, z, n, 2), HIGH, from_b)
    for dy in range(4):
        base = ((y + dy) % 4) * 2
        own = pl.ds(pl.multiple_of((base + c) * ROWS, ROWS), ROWS)
        peer = pl.ds(pl.multiple_of((base + 1 - c) * ROWS, ROWS), ROWS)
        mine[dy * ROWS:(dy + 1) * ROWS, :] = acc[own, :].astype(BF)
        other[dy * ROWS:(dy + 1) * ROWS, :] = acc[peer, :].astype(BF)


def late_call(rows, cols, values, start, parts_a, parts_b):
    part = jax.ShapeDtypeStruct((4 * ROWS, F), BF)
    return pl.pallas_call(
        late_kernel,
        out_shape=[part] * 2,
        in_specs=[smem(), smem()] + [vmem()] * 6,
        out_specs=[vmem()] * 2,
        scratch_shapes=[pltpu.VMEM((8 * ROWS, F), F32)],
        compiler_params=pltpu.CompilerParams(vmem_limit_bytes=32 * MIB),
        cost_estimate=pl.CostEstimate(
            flops=32 * 2 * BLK * BLK * F, bytes_accessed=8 * MIB, transcendentals=0
        ),
        name="backward_late",
    )(rows, cols, values, start, *parts_a, *parts_b)


def pair_kernel(mine, other, *outs):
    for n, out in enumerate(outs):
        here = pl.ds(n * ROWS, ROWS)
        out[...] = (mine[here, :].astype(F32) + other[here, :].astype(F32)).astype(BF)


def pair_call(mine, other):
    out = jax.ShapeDtypeStruct((ROWS, F), BF)
    return pl.pallas_call(
        pair_kernel,
        out_shape=[out] * 4,
        in_specs=[vmem()] * 2,
        out_specs=[vmem()] * 4,
        compiler_params=pltpu.CompilerParams(vmem_limit_bytes=24 * MIB),
        cost_estimate=pl.CostEstimate(
            flops=4 * ROWS * F, bytes_accessed=24 * ROWS * F, transcendentals=0
        ),
        name="pair_sum",
    )(mine, other)


def along_col(value, dx, dz):
    pairs = [
        (a * 4 + b, ((a + dx) % 4) * 4 + (b + dz) % 4) for a in range(4) for b in range(4)
    ]
    return lax.ppermute(value, "col", pairs)


def along_row(value, dy, dc):
    pairs = [
        (a * 2 + b, ((a + dy) % 4) * 2 + (b + dc) % 2) for a in range(4) for b in range(2)
    ]
    return lax.ppermute(value, "row", pairs)


def partner_sum(value, dx, dz):
    pairs = [(a * 4 + b, (a ^ dx) * 4 + (b ^ dz)) for a in range(4) for b in range(4)]
    return value + lax.ppermute(value, "col", pairs)


def shards(x_feat, block_values, block_rows, block_cols, weight, bias, cotangent):
    scale = 1.0 / math.sqrt(65536)

    near = {d: along_row(x_feat, d, 0) for d in (2, 1, 3)}
    swap = [along_row(x_feat, 0, 1)] + [None] * 3
    own, values, rows, cols, weight, bias, cotangent = prologue_call(
        [
            x_feat,
            block_values.reshape(128, BLK, BLK),
            block_rows.reshape(1, 128),
            block_cols.reshape(1, 128),
            weight,
            bias.reshape(1, F),
            cotangent,
        ]
    )
    near[1], own = lax.optimization_barrier((near[1], own))
    for d in (1, 3, 2):
        swap[d] = along_row(near[d], 0, 1)
    pieces = [own, near[1], near[2], near[3]] + swap

    panel, far_a1, far_a2, far_b1, far_b2 = far_call(rows, cols, values, pieces)
    extra = [
        along_col(far_a1, 1, 0),
        along_col(far_a2, 3, 0),
        along_col(far_b1, 0, 1),
        along_col(far_b2, 0, 3),
    ]
    a0, a1, a3, b0, b1, b3 = near_call(rows, cols, values, panel)
    a1, a3, b1, b3 = relay_call([a1, a3, b1, b3], extra)
    sums = stage_call(
        [a0, along_col(a1, 1, 0), along_col(a3, 3, 0)],
        [b0, along_col(b1, 0, 1), along_col(b3, 0, 3)],
    )
    sum_a, sum_b = sums[:4], sums[4:]
    part_a, part_b = [sum_a[0]] + [None] * 3, [sum_b[0]] + [None] * 3
    for d in (2, 1, 3):
        part_a[d] = along_col(sum_a[d], 0, d)
        part_b[d] = along_col(sum_b[d], d, 0)
    out_act, grad_a, grad_b, gradients = point_call(
        part_a, part_b, weight, bias, cotangent, scale
    )

    first_a, first_b = [grad_a] + [None] * 3, [grad_b] + [None] * 3
    for d in (2, 1, 3):
        first_a[d] = along_col(grad_a, 0, d)
        first_b[d] = along_col(grad_b, d, 0)
    spread = lax.all_to_all(gradients, "row", 0, 0)
    join_a, join_b, piece = join_call(first_a, first_b, spread)
    a1, a3 = along_col(join_a, 1, 0), along_col(join_a, 3, 0)
    b1, b3 = along_col(join_b, 0, 1), along_col(join_b, 0, 3)
    piece = partner_sum(partner_sum(piece, 1, 0), 2, 0)
    a1, a3, b1, b3, piece = lax.optimization_barrier((a1, a3, b1, b3, piece))
    cut_a1, cut_a3, cut_b1, cut_b3 = cut_call([a1, a3, b1, b3])
    far = [
        along_col(cut_a1, 1, 0),
        along_col(cut_a3, 3, 0),
        along_col(cut_b1, 0, 1),
        along_col(cut_b3, 0, 3),
    ]
    start = early_call(rows, cols, values, [join_a, a1, a3], [join_b, b1, b3])
    piece = partner_sum(partner_sum(piece, 0, 1), 0, 2)
    *far, piece = lax.optimization_barrier((*far, piece))
    mine, other = late_call(rows, cols, values, start, far[:2], far[2:])
    held = jnp.stack([piece] + [along_row(piece, d, 0) for d in (1, 2, 3)])
    other = along_row(other, 0, 1)
    sums = pair_call(mine, other)
    theirs = along_row(held, 0, 1)
    last = [sums[0]] + [None] * 3
    for d in (2, 1, 3):
        last[d] = along_row(sums[d], d, 0)
    x_grad, weight_grad, bias_grad = last_call(last, held, theirs)
    return (out_act, x_grad, weight_grad, bias_grad.reshape(F))


def solution(mesh):
    placed = (
        P(("row", "col"), None),
        P("row", "col", None, None, None),
        P("row", "col", None),
        P("row", "col", None),
        P(),
        P(),
        P(("row", "col"), None),
    )
    return jax.shard_map(
        shards,
        mesh=mesh,
        in_specs=placed,
        out_specs=(P(("row", "col"), None), P(("row", "col"), None), P(), P()),
        check_vma=False,
    )
```

```python
import math

import jax
import jax.numpy as jnp
from jax import lax
from jax.experimental import pallas as pl
from jax.experimental.pallas import tpu as pltpu
from jax.sharding import PartitionSpec as P

BF = jnp.bfloat16
F32 = jnp.float32
BLK = 128
PB = 4
ROWS = 512
HALF = 128
F = 256
GRP = 8
MIB = 1 << 20


def vmem():
    return pl.BlockSpec(memory_space=pltpu.VMEM)


def smem():
    return pl.BlockSpec(memory_space=pltpu.SMEM)


def hbm():
    return pl.BlockSpec(memory_space=pl.ANY)


def coords():
    row = lax.axis_index("row")
    col = lax.axis_index("col")
    y, c = row // 2, row % 2
    x, z = col // 4, col % 4
    return x + c * (z - x), z + c * (x - z), y, c


def group_at(u, v, c):
    return u * (4 - 3 * c) + v * (1 + 3 * c)


def shard_ahead(y, c, d):
    return ((y + 4 + (1 - 2 * c) * d) % 4) * 2 + c


def prologue_kernel(*refs):
    count = (len(refs) - 1) // 2
    sems = refs[-1]
    copies = [
        pltpu.make_async_copy(refs[n], refs[count + n], sems.at[n]) for n in range(count)
    ]
    for copy in copies:
        copy.start()
    for copy in copies:
        copy.wait()


def prologue_call(arrays):
    return pl.pallas_call(
        prologue_kernel,
        out_shape=[jax.ShapeDtypeStruct(a.shape, a.dtype) for a in arrays],
        in_specs=[pl.BlockSpec(memory_space=pltpu.HBM)] * len(arrays),
        out_specs=[vmem()] * len(arrays),
        scratch_shapes=[pltpu.SemaphoreType.DMA((len(arrays),))],
        compiler_params=pltpu.CompilerParams(vmem_limit_bytes=8 * MIB),
        cost_estimate=pl.CostEstimate(
            flops=0, bytes_accessed=10 * MIB, transcendentals=0
        ),
        name="prologue",
    )(*arrays)


def forward_group(rows, cols, values, panel, acc, group, lanes):
    acc[:, lanes] = jnp.zeros_like(acc[:, lanes])
    for k in range(GRP):
        local = rows[0, group * GRP + k] - group * PB
        block = cols[0, group * GRP + k]
        here = pl.ds(pl.multiple_of(local * BLK, BLK), BLK)
        there = pl.ds(pl.multiple_of(block * BLK, BLK), BLK)
        acc[here, lanes] += jnp.dot(
            values[group * GRP + k], panel[there, lanes], preferred_element_type=F32
        )


def target_group(u, v, c, p, r):
    return group_at((u + p) % 4, (v + r) % 4, c)


LOW, HIGH, ALL = slice(0, HALF), slice(HALF, F), slice(0, F)


def far_kernel(rows, cols, values, *refs):
    pieces = refs[:8]
    panel = refs[8]
    outs_a = refs[9:11]
    outs_b = refs[11:13]
    acc, sems = refs[13:]
    u, v, y, c = coords()
    copies = []
    for n in range(8):
        dy, dc = n % 4, n // 4
        shard = shard_ahead(y, c, -dy) if dc == 0 else shard_ahead(y, 1 - c, -dy)
        copies.append(
            pltpu.make_async_copy(
                pieces[n], panel.at[pl.ds(shard * ROWS, ROWS)], sems.at[n]
            )
        )
    for copy in copies:
        copy.start()
    for copy in copies:
        copy.wait()
    for n in range(4):
        lanes = ALL if n == 2 else LOW
        forward_group(rows, cols, values, panel, acc, target_group(u, v, c, 2, n), lanes)
        here = pl.ds((n % 2) * ROWS, ROWS)
        outs_a[n // 2][here, :] = acc[:, LOW].astype(BF)
        if n == 2:
            outs_b[n // 2][here, :] = acc[:, HIGH].astype(BF)
    for n in (0, 1, 3):
        forward_group(rows, cols, values, panel, acc, target_group(u, v, c, n, 2), HIGH)
        here = pl.ds((n % 2) * ROWS, ROWS)
        outs_b[n // 2][here, :] = acc[:, HIGH].astype(BF)


def far_call(rows, cols, values, pieces):
    part = jax.ShapeDtypeStruct((2 * ROWS, HALF), BF)
    return pl.pallas_call(
        far_kernel,
        out_shape=[jax.ShapeDtypeStruct((8 * ROWS, F), BF)] + [part] * 4,
        in_specs=[smem(), smem(), vmem()] + [hbm()] * 8,
        out_specs=[vmem()] * 5,
        scratch_shapes=[pltpu.VMEM((ROWS, F), F32), pltpu.SemaphoreType.DMA((8,))],
        compiler_params=pltpu.CompilerParams(vmem_limit_bytes=24 * MIB),
        cost_estimate=pl.CostEstimate(
            flops=32 * 2 * BLK * BLK * F, bytes_accessed=7 * MIB, transcendentals=0
        ),
        name="forward_far",
    )(rows, cols, values, *pieces)


def near_kernel(rows, cols, values, panel, *refs):
    outs_a = (refs[0], refs[1], None, refs[2])
    outs_b = (refs[3], refs[4], None, refs[5])
    acc = refs[6]
    u, v, y, c = coords()
    for p in (1, 3, 0, 2):
        for r in (1, 3, 0, 2):
            if p == 2 and r == 2:
                continue
            lanes = HIGH if p == 2 else LOW if r == 2 else ALL
            forward_group(rows, cols, values, panel, acc, target_group(u, v, c, p, r), lanes)
            if p != 2:
                outs_a[p][r * ROWS:(r + 1) * ROWS, :] = acc[:, LOW].astype(BF)
            if r != 2:
                outs_b[r][p * ROWS:(p + 1) * ROWS, :] = acc[:, HIGH].astype(BF)


def near_call(rows, cols, values, panel):
    part = jax.ShapeDtypeStruct((4 * ROWS, HALF), BF)
    return pl.pallas_call(
        near_kernel,
        out_shape=[part] * 6,
        in_specs=[smem(), smem(), vmem(), vmem()],
        out_specs=[vmem()] * 6,
        scratch_shapes=[pltpu.VMEM((ROWS, F), F32)],
        compiler_params=pltpu.CompilerParams(vmem_limit_bytes=24 * MIB),
        cost_estimate=pl.CostEstimate(
            flops=96 * 2 * BLK * BLK * F, bytes_accessed=9 * MIB, transcendentals=0
        ),
        name="forward_near",
    )(rows, cols, values, panel)


def relay_kernel(*refs):
    for n in range(4):
        own, extra, out = refs[n], refs[4 + n], refs[8 + n]
        mixed = pl.ds((n % 2) * 2 * ROWS, 2 * ROWS)
        plain = pl.ds((1 - n % 2) * 2 * ROWS, 2 * ROWS)
        out[mixed, :] = (own[mixed, :].astype(F32) + extra[...].astype(F32)).astype(BF)
        out[plain, :] = own[plain, :]


def relay_call(own, extra):
    return pl.pallas_call(
        relay_kernel,
        out_shape=[jax.ShapeDtypeStruct((4 * ROWS, HALF), BF)] * 4,
        in_specs=[vmem()] * 8,
        out_specs=[vmem()] * 4,
        compiler_params=pltpu.CompilerParams(vmem_limit_bytes=24 * MIB),
        cost_estimate=pl.CostEstimate(
            flops=8 * ROWS * HALF, bytes_accessed=5 * MIB, transcendentals=0
        ),
        name="relay_sum",
    )(*own, *extra)


def quad(parts, here=slice(None)):
    p0, p1, p2, p3 = (part[here].astype(F32) for part in parts)
    return (p0 + p2) + (p1 + p3)


def stage_kernel(*refs):
    for half in range(2):
        parts = refs[3 * half:3 * half + 3]
        outs = refs[6 + 4 * half:10 + 4 * half]
        for n, out in enumerate(outs):
            here = pl.ds(n * ROWS, ROWS)
            p0, p1, p3 = (part[here, :].astype(F32) for part in parts)
            out[...] = (p0 + (p1 + p3)).astype(BF)


def stage_call(parts_a, parts_b):
    return pl.pallas_call(
        stage_kernel,
        out_shape=[jax.ShapeDtypeStruct((ROWS, HALF), BF)] * 8,
        in_specs=[vmem()] * 6,
        out_specs=[vmem()] * 8,
        compiler_params=pltpu.CompilerParams(vmem_limit_bytes=24 * MIB),
        cost_estimate=pl.CostEstimate(
            flops=24 * ROWS * HALF, bytes_accessed=4 * MIB, transcendentals=0
        ),
        name="stage_sum",
    )(*parts_a, *parts_b)


def point_kernel(scale, *refs):
    parts_a = refs[:4]
    parts_b = refs[4:8]
    weight, bias, cotangent = refs[8:11]
    out_act, grad_a, grad_b, keep, give, full = refs[11:]
    u, v, y, c = coords()

    aggregated = jnp.concatenate(
        [quad(parts_a).astype(BF), quad(parts_b).astype(BF)], axis=1
    )
    pre = jnp.dot(aggregated, weight[...], preferred_element_type=F32) + bias[...]
    gate = jax.nn.sigmoid(pre)
    out_act[...] = (pre * gate).astype(BF)
    grad_pre = (
        cotangent[...].astype(F32) * gate * (1.0 + pre * (1.0 - gate))
    ).astype(BF)
    grad_agg = lax.dot_general(
        grad_pre, weight[...], (((1,), (1,)), ((), ())), preferred_element_type=F32
    ).astype(BF)
    grad_a[...] = grad_agg[:, :HALF]
    grad_b[...] = grad_agg[:, HALF:]
    full[...] = lax.dot_general(
        aggregated, grad_pre, (((0,), (0,)), ((), ())), preferred_element_type=F32
    ) * scale
    bias_grad = jnp.sum(grad_pre.astype(F32), axis=0, keepdims=True) * scale
    for out, core in ((keep, c), (give, 1 - c)):
        out[:HALF, :] = full[pl.ds(pl.multiple_of(core * HALF, HALF), HALF), :]
        out[HALF:, :] = jnp.broadcast_to(bias_grad, (8, F))


def point_call(parts_a, parts_b, weight, bias, cotangent, scale):
    half = jax.ShapeDtypeStruct((ROWS, HALF), BF)
    return pl.pallas_call(
        lambda *refs: point_kernel(scale, *refs),
        out_shape=[
            jax.ShapeDtypeStruct((ROWS, F), BF),
            half,
            half,
            jax.ShapeDtypeStruct((HALF + 8, F), F32),
            jax.ShapeDtypeStruct((HALF + 8, F), F32),
        ],
        in_specs=[vmem()] * 11,
        out_specs=[vmem()] * 5,
        scratch_shapes=[pltpu.VMEM((F, F), F32)],
        compiler_params=pltpu.CompilerParams(vmem_limit_bytes=24 * MIB),
        cost_estimate=pl.CostEstimate(
            flops=3 * 2 * ROWS * F * F, bytes_accessed=2 * MIB, transcendentals=ROWS * F
        ),
        name="pointwise",
    )(*parts_a, *parts_b, weight, bias, cotangent)


def join_kernel(*refs):
    outs = refs[10:12]
    for half in range(2):
        for n in range(4):
            outs[half][n * ROWS:(n + 1) * ROWS, :] = refs[4 * half + n][...]
    refs[12][...] = refs[8][...] + refs[9][...]


def join_call(parts_a, parts_b, keep, got):
    return pl.pallas_call(
        join_kernel,
        out_shape=[jax.ShapeDtypeStruct((4 * ROWS, HALF), BF)] * 2
        + [jax.ShapeDtypeStruct(keep.shape, F32)],
        in_specs=[vmem()] * 10,
        out_specs=[vmem()] * 3,
        compiler_params=pltpu.CompilerParams(vmem_limit_bytes=8 * MIB),
        cost_estimate=pl.CostEstimate(
            flops=136 * F, bytes_accessed=3 * MIB, transcendentals=0
        ),
        name="join",
    )(*parts_a, *parts_b, keep, got)


def cut_kernel(*refs):
    for n in range(4):
        refs[4 + n][...] = refs[n][pl.ds((n % 2) * 2 * ROWS, 2 * ROWS), :]


def cut_call(parts):
    return pl.pallas_call(
        cut_kernel,
        out_shape=[jax.ShapeDtypeStruct((2 * ROWS, HALF), BF)] * 4,
        in_specs=[vmem()] * 4,
        out_specs=[vmem()] * 4,
        compiler_params=pltpu.CompilerParams(vmem_limit_bytes=16 * MIB),
        cost_estimate=pl.CostEstimate(
            flops=0, bytes_accessed=2 * MIB, transcendentals=0
        ),
        name="cut",
    )(*parts)


def last_kernel(*refs):
    mine, theirs, x_grad, weight_grad, bias_grad = refs[4:]
    u, v, y, c = coords()
    x_grad[...] = quad(refs[:4]).astype(BF)
    for source, core in ((mine, c), (theirs, 1 - c)):
        here = pl.ds(pl.multiple_of(core * HALF, HALF), HALF)
        weight_grad[here, :] = source[:HALF, :]

        @pl.when(core == 0)
        def _(source=source):
            bias_grad[...] = source[HALF:HALF + 1, :]


def last_call(parts, mine, theirs):
    return pl.pallas_call(
        last_kernel,
        out_shape=[
            jax.ShapeDtypeStruct((ROWS, F), BF),
            jax.ShapeDtypeStruct((F, F), F32),
            jax.ShapeDtypeStruct((1, F), F32),
        ],
        in_specs=[vmem()] * 6,
        out_specs=[vmem()] * 3,
        compiler_params=pltpu.CompilerParams(vmem_limit_bytes=8 * MIB),
        cost_estimate=pl.CostEstimate(
            flops=4 * ROWS * F, bytes_accessed=10 * ROWS * F, transcendentals=0
        ),
        name="last_sum",
    )(*parts, mine, theirs)


def backward_slots(rows, cols, values, acc, group, lanes, read):
    for k in range(GRP):
        local = rows[0, group * GRP + k] - group * PB
        there = pl.ds(pl.multiple_of(cols[0, group * GRP + k] * BLK, BLK), BLK)
        acc[there, lanes] += lax.dot_general(
            values[group * GRP + k],
            read(local),
            (((0,), (0,)), ((), ())),
            preferred_element_type=F32,
        )


def source_group(u, v, c, p, r):
    return group_at((u + 4 - p) % 4, (v + 4 - r) % 4, c)


def block_at(base, local):
    return pl.ds(pl.multiple_of(base + local * BLK, BLK), BLK)


def early_kernel(rows, cols, values, *refs):
    parts_a = (refs[0], refs[1], None, refs[2])
    parts_b = (refs[3], refs[4], None, refs[5])
    acc = refs[6]
    u, v, y, c = coords()
    acc[...] = jnp.zeros_like(acc)
    for p in range(4):
        for r in range(4):
            if p == 2 and r == 2:
                continue

            def from_a(local, p=p, r=r):
                return parts_a[p][block_at(r * ROWS, local), :]

            def from_b(local, p=p, r=r):
                return parts_b[r][block_at(p * ROWS, local), :]

            def both(local, from_a=from_a, from_b=from_b):
                return jnp.concatenate([from_a(local), from_b(local)], axis=1)

            lanes, read = (HIGH, from_b) if p == 2 else (LOW, from_a) if r == 2 else (ALL, both)
            backward_slots(rows, cols, values, acc, source_group(u, v, c, p, r), lanes, read)


def early_call(rows, cols, values, parts_a, parts_b):
    return pl.pallas_call(
        early_kernel,
        out_shape=jax.ShapeDtypeStruct((8 * ROWS, F), F32),
        in_specs=[smem(), smem()] + [vmem()] * 7,
        out_specs=vmem(),
        compiler_params=pltpu.CompilerParams(vmem_limit_bytes=24 * MIB),
        cost_estimate=pl.CostEstimate(
            flops=96 * 2 * BLK * BLK * F, bytes_accessed=10 * MIB, transcendentals=0
        ),
        name="backward_early",
    )(rows, cols, values, *parts_a, *parts_b)


def late_kernel(rows, cols, values, start, *refs):
    parts_a = refs[:2]
    parts_b = refs[2:4]
    mine, other, acc = refs[4:]
    u, v, y, c = coords()
    acc[...] = start[...]
    for n in range(4):

        def from_a(local, n=n):
            return parts_a[n // 2][block_at((n % 2) * ROWS, local), :]

        def from_b(local, n=n):
            return parts_b[n // 2][block_at((n % 2) * ROWS, local), :]

        backward_slots(rows, cols, values, acc, source_group(u, v, c, 2, n), LOW, from_a)
        backward_slots(rows, cols, values, acc, source_group(u, v, c, n, 2), HIGH, from_b)
    for dy in range(4):
        own = pl.ds(pl.multiple_of(shard_ahead(y, c, dy) * ROWS, ROWS), ROWS)
        peer = pl.ds(pl.multiple_of(shard_ahead(y, 1 - c, dy) * ROWS, ROWS), ROWS)
        mine[dy * ROWS:(dy + 1) * ROWS, :] = acc[own, :].astype(BF)
        other[dy * ROWS:(dy + 1) * ROWS, :] = acc[peer, :].astype(BF)


def late_call(rows, cols, values, start, parts_a, parts_b):
    part = jax.ShapeDtypeStruct((4 * ROWS, F), BF)
    return pl.pallas_call(
        late_kernel,
        out_shape=[part] * 2,
        in_specs=[smem(), smem()] + [vmem()] * 6,
        out_specs=[vmem()] * 2,
        scratch_shapes=[pltpu.VMEM((8 * ROWS, F), F32)],
        compiler_params=pltpu.CompilerParams(vmem_limit_bytes=32 * MIB),
        cost_estimate=pl.CostEstimate(
            flops=32 * 2 * BLK * BLK * F, bytes_accessed=8 * MIB, transcendentals=0
        ),
        name="backward_late",
    )(rows, cols, values, start, *parts_a, *parts_b)


def pair_kernel(mine, other, *outs):
    for n, out in enumerate(outs):
        here = pl.ds(n * ROWS, ROWS)
        out[...] = (mine[here, :].astype(F32) + other[here, :].astype(F32)).astype(BF)


def pair_call(mine, other):
    out = jax.ShapeDtypeStruct((ROWS, F), BF)
    return pl.pallas_call(
        pair_kernel,
        out_shape=[out] * 4,
        in_specs=[vmem()] * 2,
        out_specs=[vmem()] * 4,
        compiler_params=pltpu.CompilerParams(vmem_limit_bytes=24 * MIB),
        cost_estimate=pl.CostEstimate(
            flops=4 * ROWS * F, bytes_accessed=24 * ROWS * F, transcendentals=0
        ),
        name="pair_sum",
    )(mine, other)


def permute(value, target):
    pairs = []
    for row in range(8):
        for col in range(16):
            y, c = row // 2, row % 2
            x, z = col // 4, col % 4
            u, v = (z, x) if c else (x, z)
            u, v, y, c = target(u, v, y, c)
            x, z = (v, u) if row % 2 else (u, v)
            pairs.append((row * 16 + col, (y * 2 + c) * 16 + x * 4 + z))
    return lax.ppermute(value, ("row", "col"), pairs)


def along_u(value, d):
    return permute(value, lambda u, v, y, c: ((u + d) % 4, v, y, c))


def along_v(value, d):
    return permute(value, lambda u, v, y, c: (u, (v + d) % 4, y, c))


def along_y(value, d):
    return permute(value, lambda u, v, y, c: (u, v, (y + (1 - 2 * c) * d) % 4, c))


def to_peer(value):
    return permute(value, lambda u, v, y, c: (u, v, y, 1 - c))


def with_u(value, d):
    return value + permute(value, lambda u, v, y, c: (u ^ d, v, y, c))


def with_v(value, d):
    return value + permute(value, lambda u, v, y, c: (u, v ^ d, y, c))


def with_y(value, d):
    return value + permute(value, lambda u, v, y, c: (u, v, y ^ d, c))


def shards(x_feat, block_values, block_rows, block_cols, weight, bias, cotangent):
    scale = 1.0 / math.sqrt(65536)

    near = {d: along_y(x_feat, d) for d in (2, 1, 3)}
    swap = [to_peer(x_feat)] + [None] * 3
    own, values, rows, cols, weight, bias, cotangent = prologue_call(
        [
            x_feat,
            block_values.reshape(128, BLK, BLK),
            block_rows.reshape(1, 128),
            block_cols.reshape(1, 128),
            weight,
            bias.reshape(1, F),
            cotangent,
        ]
    )
    near[1], own = lax.optimization_barrier((near[1], own))
    for d in (1, 3, 2):
        swap[d] = to_peer(near[d])
    pieces = [own, near[1], near[2], near[3]] + swap

    panel, far_a1, far_a2, far_b1, far_b2 = far_call(rows, cols, values, pieces)
    extra = [
        along_u(far_a1, 1),
        along_u(far_a2, 3),
        along_v(far_b1, 1),
        along_v(far_b2, 3),
    ]
    a0, a1, a3, b0, b1, b3 = near_call(rows, cols, values, panel)
    a1, a3, b1, b3 = relay_call([a1, a3, b1, b3], extra)
    sums = stage_call(
        [a0, along_u(a1, 1), along_u(a3, 3)],
        [b0, along_v(b1, 1), along_v(b3, 3)],
    )
    sum_a, sum_b = sums[:4], sums[4:]
    part_a, part_b = [sum_a[0]] + [None] * 3, [sum_b[0]] + [None] * 3
    for d in (2, 1, 3):
        part_a[d] = along_v(sum_a[d], d)
        part_b[d] = along_u(sum_b[d], d)
    out_act, grad_a, grad_b, keep, give = point_call(
        part_a, part_b, weight, bias, cotangent, scale
    )

    first_a, first_b = [grad_a] + [None] * 3, [grad_b] + [None] * 3
    for d in (2, 1, 3):
        first_a[d] = along_v(grad_a, d)
        first_b[d] = along_u(grad_b, d)
    join_a, join_b, piece = join_call(first_a, first_b, keep, to_peer(give))
    a1, a3 = along_u(join_a, 1), along_u(join_a, 3)
    b1, b3 = along_v(join_b, 1), along_v(join_b, 3)
    piece = with_y(with_y(piece, 1), 2)
    a1, a3, b1, b3, piece = lax.optimization_barrier((a1, a3, b1, b3, piece))
    cut_a1, cut_a3, cut_b1, cut_b3 = cut_call([a1, a3, b1, b3])
    far = [
        along_u(cut_a1, 1),
        along_u(cut_a3, 3),
        along_v(cut_b1, 1),
        along_v(cut_b3, 3),
    ]
    piece = with_u(piece, 1)
    start = early_call(rows, cols, values, [join_a, a1, a3], [join_b, b1, b3])
    piece, start = lax.optimization_barrier((piece, start))
    piece = with_u(piece, 2)
    mine, other = late_call(rows, cols, values, start, far[:2], far[2:])
    piece, other = lax.optimization_barrier((piece, other))
    other = to_peer(other)
    piece = with_v(piece, 1)
    other, piece = lax.optimization_barrier((other, piece))
    sums = pair_call(mine, other)
    last = [sums[0]] + [None] * 3
    for d in (2, 1, 3):
        last[d] = along_y(sums[d], d)
    piece = with_v(piece, 2)
    x_grad, weight_grad, bias_grad = last_call(last, piece, to_peer(piece))
    return (out_act, x_grad, weight_grad, bias_grad.reshape(F))


def solution(mesh):
    placed = (
        P(("row", "col"), None),
        P("row", "col", None, None, None),
        P("row", "col", None),
        P("row", "col", None),
        P(),
        P(),
        P(("row", "col"), None),
    )
    return jax.shard_map(
        shards,
        mesh=mesh,
        in_specs=placed,
        out_specs=(P(("row", "col"), None), P(("row", "col"), None), P(), P()),
        check_vma=False,
    )
```

```python
import math

import jax
import jax.numpy as jnp
from jax import lax
from jax.experimental import pallas as pl
from jax.experimental.pallas import tpu as pltpu
from jax.sharding import PartitionSpec as P

BF = jnp.bfloat16
F32 = jnp.float32
BLK = 128
PB = 4
ROWS = 512
HALF = 128
F = 256
GRP = 8
MIB = 1 << 20


def vmem():
    return pl.BlockSpec(memory_space=pltpu.VMEM)


def smem():
    return pl.BlockSpec(memory_space=pltpu.SMEM)


def hbm():
    return pl.BlockSpec(memory_space=pl.ANY)


def coords():
    row = lax.axis_index("row")
    col = lax.axis_index("col")
    y, c = row // 2, row % 2
    x, z = col // 4, col % 4
    return x + c * (z - x), z + c * (x - z), y, c


def group_at(u, v, c):
    return u * (4 - 3 * c) + v * (1 + 3 * c)


def ahead(y, c, d):
    return (y + 4 + (1 - 2 * c) * d) % 4


def target_group(u, v, c, p, r):
    return group_at((u + p) % 4, (v + r) % 4, c)


def source_group(u, v, c, p, r):
    return group_at((u + 4 - p) % 4, (v + 4 - r) % 4, c)


def local_call(kernel, name, ins, outs, args, limit, flops=0, moved=MIB, scratch=()):
    return pl.pallas_call(
        kernel,
        out_shape=outs,
        in_specs=ins,
        out_specs=[vmem()] * len(outs),
        scratch_shapes=list(scratch),
        compiler_params=pltpu.CompilerParams(vmem_limit_bytes=limit * MIB),
        cost_estimate=pl.CostEstimate(
            flops=flops, bytes_accessed=moved, transcendentals=0
        ),
        name=name,
    )(*args)


def shape(rows, width=HALF, dtype=BF):
    return jax.ShapeDtypeStruct((rows, width), dtype)


def lanes_of(core):
    return pl.ds(pl.multiple_of(core * HALF, HALF), HALF)


def rows_at(start, size):
    return pl.ds(pl.multiple_of(start, size), size)


def split_kernel(x_feat, keep, give):
    u, v, y, c = coords()
    keep[...] = x_feat[:, lanes_of(c)]
    give[...] = x_feat[:, lanes_of(1 - c)]


def ids_kernel(rows, cols, ids):
    ids[0:1, :] = rows[...]
    ids[1:2, :] = cols[...]


def stack_kernel(*refs):
    size = refs[0].shape[0]
    for n, ref in enumerate(refs[:-1]):
        refs[-1][n * size:(n + 1) * size, :] = ref[...]


def stack_call(parts, name):
    size, width = parts[0].shape
    return local_call(
        stack_kernel, name, [vmem()] * len(parts), [shape(size * len(parts), width)],
        parts, 8,
    )[0]


def prologue_kernel(*refs):
    count = (len(refs) - 1) // 2
    sems = refs[-1]
    copies = [
        pltpu.make_async_copy(refs[n], refs[count + n], sems.at[n]) for n in range(count)
    ]
    for copy in copies:
        copy.start()
    for copy in copies:
        copy.wait()


def prologue_call(arrays):
    return local_call(
        prologue_kernel, "prologue", [hbm()] * len(arrays),
        [jax.ShapeDtypeStruct(a.shape, a.dtype) for a in arrays], arrays, 8,
        moved=10 * MIB, scratch=[pltpu.SemaphoreType.DMA((len(arrays),))],
    )


def forward_group(ids, values, panel, acc, group):
    acc[...] = jnp.zeros_like(acc)
    for k in range(GRP):
        slot = group * GRP + k
        here = rows_at((ids[0, slot] - group * PB) * BLK, BLK)
        there = rows_at(ids[1, slot] * BLK, BLK)
        acc[here, :] += jnp.dot(
            values[slot], panel[there, :], preferred_element_type=F32
        )


def far_kernel(*refs):
    tiles = (refs[0:2], refs[2:4])
    pieces = refs[4:8]
    panel, low, high, acc, sems = refs[8:]
    u, v, y, c = coords()
    copies = []
    for n in range(8):
        d, t = n // 2, n % 2
        shard = ahead(y, c, -d) * 2 + (c if t == 0 else 1 - c)
        copies.append(
            pltpu.make_async_copy(
                pieces[d].at[pl.ds(t * ROWS, ROWS)],
                panel.at[rows_at(shard * ROWS, ROWS)],
                sems.at[n],
            )
        )
    for copy in copies:
        copy.start()
    for copy in copies:
        copy.wait()
    for r in range(4):
        for t in range(2):
            ids, values = tiles[t]
            forward_group(ids, values, panel, acc.at[t], target_group(u, v, c, 2, r))
            start = ((r % 2) * 2 + t) * ROWS
            (low, high)[r // 2][start:start + ROWS, :] = acc[t].astype(BF)


def near_kernel(*refs):
    tiles = (refs[0:2], refs[2:4])
    panel = refs[4]
    outs = dict(zip((1, 3, 0), refs[5:8]))
    acc = refs[8]
    u, v, y, c = coords()
    for p, out in outs.items():
        for r in range(4):
            for t in range(2):
                ids, values = tiles[t]
                forward_group(ids, values, panel, acc.at[t], target_group(u, v, c, p, r))
                start = (r * 2 + t) * ROWS
                out[start:start + ROWS, :] = acc[t].astype(BF)


def relay_kernel(*refs):
    for n in range(2):
        own, extra, out = refs[n], refs[2 + n], refs[4 + n]
        mixed = pl.ds(n * 4 * ROWS, 4 * ROWS)
        plain = pl.ds((1 - n) * 4 * ROWS, 4 * ROWS)
        out[mixed, :] = (own[mixed, :].astype(F32) + extra[...].astype(F32)).astype(BF)
        out[plain, :] = own[plain, :]


def stage_kernel(*refs):
    for n, out in enumerate(refs[3:]):
        here = pl.ds(n * 2 * ROWS, 2 * ROWS)
        p0, p1, p3 = (part[here, :].astype(F32) for part in refs[:3])
        out[...] = (p0 + (p1 + p3)).astype(BF)


def quad(parts, here):
    p0, p1, p2, p3 = (part[here, :].astype(F32) for part in parts)
    return (p0 + p2) + (p1 + p3)


def finish_kernel(*refs):
    refs[4][...] = quad(refs[:4], pl.ds(0, ROWS)).astype(BF)
    refs[5][...] = quad(refs[:4], pl.ds(ROWS, ROWS)).astype(BF)


def finish_call(parts, name):
    return local_call(
        finish_kernel, name, [vmem()] * 4, [shape(ROWS)] * 2, parts, 8,
        flops=8 * ROWS * HALF,
    )


def point_kernel(scale, *refs):
    own, peer, weight, bias, cotangent = refs[:5]
    out_act, keep_g, give_g, keep_w, give_w, whole, grads, full = refs[5:]
    u, v, y, c = coords()
    whole[:, lanes_of(c)] = own[...]
    whole[:, lanes_of(1 - c)] = peer[...]
    aggregated = whole[...]
    pre = jnp.dot(aggregated, weight[...], preferred_element_type=F32) + bias[...]
    gate = jax.nn.sigmoid(pre)
    out_act[...] = (pre * gate).astype(BF)
    grad_pre = (
        cotangent[...].astype(F32) * gate * (1.0 + pre * (1.0 - gate))
    ).astype(BF)
    grads[...] = lax.dot_general(
        grad_pre, weight[...], (((1,), (1,)), ((), ())), preferred_element_type=F32
    ).astype(BF)
    keep_g[...] = grads[:, lanes_of(c)]
    give_g[...] = grads[:, lanes_of(1 - c)]
    full[...] = lax.dot_general(
        aggregated, grad_pre, (((0,), (0,)), ((), ())), preferred_element_type=F32
    ) * scale
    bias_grad = jnp.sum(grad_pre.astype(F32), axis=0, keepdims=True) * scale
    for out, core in ((keep_w, c), (give_w, 1 - c)):
        out[:HALF, :] = full[rows_at(core * HALF, HALF), :]
        out[HALF:, :] = jnp.broadcast_to(bias_grad, (8, F))


def cut_kernel(left, right, low, high):
    low[...] = left[:4 * ROWS, :]
    high[...] = right[4 * ROWS:, :]


def backward_group(ids, values, acc, part, base, group):
    for k in range(GRP):
        slot = group * GRP + k
        here = rows_at(base + (ids[0, slot] - group * PB) * BLK, BLK)
        there = rows_at(ids[1, slot] * BLK, BLK)
        acc[there, :] += lax.dot_general(
            values[slot], part[here, :], (((0,), (0,)), ((), ())),
            preferred_element_type=F32,
        )


def early_kernel(*refs):
    tiles = (refs[0:2], refs[2:4])
    parts = dict(zip((0, 1, 3), refs[4:7]))
    acc = refs[7]
    u, v, y, c = coords()
    acc[...] = jnp.zeros_like(acc)
    for p, part in parts.items():
        for r in range(4):
            for t in range(2):
                ids, values = tiles[t]
                group = source_group(u, v, c, p, r)
                backward_group(ids, values, acc, part, (r * 2 + t) * ROWS, group)


def late_kernel(*refs):
    tiles = (refs[0:2], refs[2:4])
    start = refs[4]
    parts = refs[5:7]
    outs = refs[7:11]
    acc = refs[11]
    u, v, y, c = coords()
    acc[...] = start[...]
    for r in range(4):
        for t in range(2):
            ids, values = tiles[t]
            group = source_group(u, v, c, 2, r)
            base = ((r % 2) * 2 + t) * ROWS
            backward_group(ids, values, acc, parts[r // 2], base, group)
    for d in range(4):
        first = ahead(y, c, d) * 2
        for t, core in ((0, c), (1, 1 - c)):
            outs[d][t * ROWS:(t + 1) * ROWS, :] = acc[
                rows_at((first + core) * ROWS, ROWS), :
            ].astype(BF)


def sum_kernel(s0, s1, s2, s3, after, out):
    out[...] = (s0[...] + s2[...]) + (s1[...] + s3[...])


def last_kernel(own, peer, mine, theirs, x_grad, weight_grad, bias_grad):
    u, v, y, c = coords()
    x_grad[:, lanes_of(c)] = own[...]
    x_grad[:, lanes_of(1 - c)] = peer[...]
    for source, core in ((mine, c), (theirs, 1 - c)):
        weight_grad[rows_at(core * HALF, HALF), :] = source[:HALF, :]

        @pl.when(core == 0)
        def _(source=source):
            bias_grad[...] = source[HALF:HALF + 1, :]


def permute(value, target):
    pairs = []
    for row in range(8):
        for col in range(16):
            y, c = row // 2, row % 2
            x, z = col // 4, col % 4
            u, v = (z, x) if c else (x, z)
            u, v, y, c = target(u, v, y, c)
            x, z = (v, u) if row % 2 else (u, v)
            pairs.append((row * 16 + col, (y * 2 + c) * 16 + x * 4 + z))
    return lax.ppermute(value, ("row", "col"), pairs)


def along_u(value, d):
    return permute(value, lambda u, v, y, c: ((u + d) % 4, v, y, c))


def along_v(value, d):
    return permute(value, lambda u, v, y, c: (u, (v + d) % 4, y, c))


def along_y(value, d):
    return permute(value, lambda u, v, y, c: (u, v, (y + (1 - 2 * c) * d) % 4, c))


def to_peer(value):
    return permute(value, lambda u, v, y, c: (u, v, y, 1 - c))


def with_u(value, d):
    return value + permute(value, lambda u, v, y, c: (u ^ d, v, y, c))


def with_v(value, d):
    return value + permute(value, lambda u, v, y, c: (u, v ^ d, y, c))


def with_y(value, d):
    return value + permute(value, lambda u, v, y, c: (u, v, y ^ d, c))


def spread(value, along):
    others = {d: along(value, d) for d in (2, 1, 3)}
    return [value, others[1], others[2], others[3]]


def exchange(parts, along):
    others = {d: along(parts[d], d) for d in (2, 1, 3)}
    return [parts[0], others[1], others[2], others[3]]


def shards(x_feat, block_values, block_rows, block_cols, weight, bias, cotangent):
    scale = 1.0 / math.sqrt(65536)
    values = block_values.reshape(128, BLK, BLK)
    slab = 2 * 128 * BLK * BLK * HALF

    keep, give = local_call(
        split_kernel, "split", [vmem()], [shape(ROWS), shape(ROWS)], [x_feat], 4,
    )
    got = to_peer(give)
    got, values, rows, cols = lax.optimization_barrier(
        (got, values, block_rows.reshape(1, 128), block_cols.reshape(1, 128))
    )
    (ids,) = local_call(
        ids_kernel, "ids", [vmem()] * 2, [shape(2, 128, jnp.int32)], [rows, cols], 2,
        moved=2048,
    )
    pair = stack_call([keep, got], "pair")
    pieces = spread(pair, along_y)
    peer_values = to_peer(values)
    peer_ids = to_peer(ids)
    values, weight, bias, cotangent = prologue_call(
        [values, weight, bias.reshape(1, F), cotangent]
    )
    pieces[1], values = lax.optimization_barrier((pieces[1], values))
    tiles = [ids, values, peer_ids, peer_values]
    tile_specs = [smem(), vmem(), smem(), vmem()]

    panel, low, high = local_call(
        far_kernel, "forward_far", tile_specs + [hbm()] * 4,
        [shape(8 * ROWS), shape(4 * ROWS), shape(4 * ROWS)], tiles + pieces, 8,
        flops=slab // 2, moved=6 * MIB,
        scratch=[pltpu.VMEM((2, ROWS, HALF), F32), pltpu.SemaphoreType.DMA((8,))],
    )
    extra = [along_u(low, 1), along_u(high, 3)]
    p1, p3, p0 = local_call(
        near_kernel, "forward_near", tile_specs + [vmem()], [shape(8 * ROWS)] * 3,
        tiles + [panel], 8, flops=3 * slab // 2, moved=10 * MIB,
        scratch=[pltpu.VMEM((2, ROWS, HALF), F32)],
    )
    p1, p3 = local_call(
        relay_kernel, "relay_sum", [vmem()] * 4, [shape(8 * ROWS)] * 2,
        [p1, p3] + extra, 8, flops=8 * ROWS * HALF, moved=5 * MIB,
    )
    sums = local_call(
        stage_kernel, "stage_sum", [vmem()] * 3, [shape(2 * ROWS)] * 4,
        [p0, along_u(p1, 1), along_u(p3, 3)], 8, flops=16 * ROWS * HALF,
        moved=4 * MIB,
    )
    own, other = finish_call(exchange(sums, along_v), "aggregate")
    out_act, keep_g, give_g, keep_w, give_w = local_call(
        lambda *refs: point_kernel(scale, *refs), "pointwise", [vmem()] * 5,
        [shape(ROWS, F), shape(ROWS), shape(ROWS)] + [shape(HALF + 8, F, F32)] * 2,
        [own, to_peer(other), weight, bias, cotangent], 8, flops=6 * ROWS * F * F,
        moved=2 * MIB,
        scratch=[
            pltpu.VMEM((ROWS, F), BF), pltpu.VMEM((ROWS, F), BF), pltpu.VMEM((F, F), F32),
        ],
    )

    got_g = to_peer(give_g)
    piece = to_peer(give_w)
    got_g, piece = lax.optimization_barrier((got_g, piece))
    grads = stack_call([keep_g, got_g], "pair_grads")
    firsts = spread(grads, along_v)
    piece = with_y(keep_w + piece, 1)
    *firsts, piece = lax.optimization_barrier((*firsts, piece))
    join = stack_call(firsts, "join")
    left, right = along_u(join, 1), along_u(join, 3)
    piece = with_y(piece, 2)
    gate = lax.optimization_barrier((left, right, piece))
    left, right = gate[:2]
    s0, s1, s2, s3 = spread(piece, along_u)
    low, high = local_call(
        cut_kernel, "cut", [vmem()] * 2, [shape(4 * ROWS)] * 2, [left, right], 8,
    )
    far = [along_u(low, 1), along_u(high, 3)]
    (start,) = local_call(
        early_kernel, "backward_early", tile_specs + [vmem()] * 3,
        [shape(8 * ROWS, HALF, F32)], tiles + [join, left, right], 8,
        flops=3 * slab // 2, moved=10 * MIB,
    )
    outs = local_call(
        late_kernel, "backward_late", tile_specs + [vmem()] * 3, [shape(2 * ROWS)] * 4,
        tiles + [start] + far, 8, flops=slab // 2, moved=6 * MIB,
        scratch=[pltpu.VMEM((8 * ROWS, HALF), F32)],
    )
    (piece,) = local_call(
        sum_kernel, "sum_u", [vmem()] * 4 + [hbm()], [shape(HALF + 8, F, F32)],
        [s0, s1, s2, s3, outs[0]], 4,
    )
    lasts = exchange(outs, along_y)
    piece = with_v(with_v(piece, 1), 2)
    *lasts, piece = lax.optimization_barrier((*lasts, piece))
    own, other = finish_call(lasts, "sum_x")
    x_grad, weight_grad, bias_grad = local_call(
        last_kernel, "last", [vmem()] * 4,
        [shape(ROWS, F), shape(F, F, F32), shape(1, F, F32)],
        [own, to_peer(other), piece, to_peer(piece)], 8,
    )
    return (out_act, x_grad, weight_grad, bias_grad.reshape(F))


def solution(mesh):
    placed = (
        P(("row", "col"), None),
        P("row", "col", None, None, None),
        P("row", "col", None),
        P("row", "col", None),
        P(),
        P(),
        P(("row", "col"), None),
    )
    return jax.shard_map(
        shards,
        mesh=mesh,
        in_specs=placed,
        out_specs=(P(("row", "col"), None), P(("row", "col"), None), P(), P()),
        check_vma=False,
    )
```

```python
import math

import jax
import jax.numpy as jnp
from jax import lax
from jax.experimental import pallas as pl
from jax.experimental.pallas import tpu as pltpu
from jax.sharding import PartitionSpec as P

BF = jnp.bfloat16
F32 = jnp.float32
BLK = 128
PB = 4
ROWS = 512
HALF = 128
F = 256
GRP = 8
MIB = 1 << 20


def vmem():
    return pl.BlockSpec(memory_space=pltpu.VMEM)


def smem():
    return pl.BlockSpec(memory_space=pltpu.SMEM)


def hbm():
    return pl.BlockSpec(memory_space=pl.ANY)


def coords():
    row = lax.axis_index("row")
    col = lax.axis_index("col")
    y, c = row // 2, row % 2
    x, z = col // 4, col % 4
    return x + c * (z - x), z + c * (x - z), y, c


def group_at(u, v, c):
    return u * (4 - 3 * c) + v * (1 + 3 * c)


def ahead(y, c, d):
    return (y + 4 + (1 - 2 * c) * d) % 4


def target_group(u, v, c, p, r):
    return group_at((u + p) % 4, (v + r) % 4, c)


def source_group(u, v, c, p, r):
    return group_at((u + 4 - p) % 4, (v + 4 - r) % 4, c)


def local_call(kernel, name, ins, outs, args, limit, flops=0, moved=MIB, scratch=()):
    return pl.pallas_call(
        kernel,
        out_shape=outs,
        in_specs=ins,
        out_specs=[vmem()] * len(outs),
        scratch_shapes=list(scratch),
        compiler_params=pltpu.CompilerParams(vmem_limit_bytes=limit * MIB),
        cost_estimate=pl.CostEstimate(
            flops=flops, bytes_accessed=moved, transcendentals=0
        ),
        name=name,
    )(*args)


def shape(rows, width=HALF, dtype=BF):
    return jax.ShapeDtypeStruct((rows, width), dtype)


def lanes_of(core):
    return pl.ds(pl.multiple_of(core * HALF, HALF), HALF)


def rows_at(start, size):
    return pl.ds(pl.multiple_of(start, size), size)


def split_kernel(x_feat, keep, give):
    u, v, y, c = coords()
    keep[...] = x_feat[:, lanes_of(c)]
    give[...] = x_feat[:, lanes_of(1 - c)]


def ids_kernel(rows, cols, ids):
    ids[0:1, :] = rows[...]
    ids[1:2, :] = cols[...]


def stack_kernel(*refs):
    size = refs[0].shape[0]
    for n, ref in enumerate(refs[:-1]):
        refs[-1][n * size:(n + 1) * size, :] = ref[...]


def stack_call(parts, name):
    size, width = parts[0].shape
    return local_call(
        stack_kernel, name, [vmem()] * len(parts), [shape(size * len(parts), width)],
        parts, 8,
    )[0]


def prologue_kernel(*refs):
    count = (len(refs) - 1) // 2
    sems = refs[-1]
    copies = [
        pltpu.make_async_copy(refs[n], refs[count + n], sems.at[n]) for n in range(count)
    ]
    for copy in copies:
        copy.start()
    for copy in copies:
        copy.wait()


def prologue_call(arrays):
    return local_call(
        prologue_kernel, "prologue", [hbm()] * len(arrays),
        [jax.ShapeDtypeStruct(a.shape, a.dtype) for a in arrays], arrays, 8,
        moved=10 * MIB, scratch=[pltpu.SemaphoreType.DMA((len(arrays),))],
    )


def forward_group(ids, values, panel, acc, group):
    acc[...] = jnp.zeros_like(acc)
    for k in range(GRP):
        slot = group * GRP + k
        here = rows_at((ids[0, slot] - group * PB) * BLK, BLK)
        there = rows_at(ids[1, slot] * BLK, BLK)
        acc[here, :] += jnp.dot(
            values[slot], panel[there, :], preferred_element_type=F32
        )


def far_kernel(*refs):
    tiles = (refs[0:2], refs[2:4])
    pieces = refs[4:8]
    panel, low, high, acc, sems = refs[8:]
    u, v, y, c = coords()
    copies = []
    for n in range(8):
        d, t = n // 2, n % 2
        shard = ahead(y, c, -d) * 2 + (c if t == 0 else 1 - c)
        copies.append(
            pltpu.make_async_copy(
                pieces[d].at[pl.ds(t * ROWS, ROWS)],
                panel.at[rows_at(shard * ROWS, ROWS)],
                sems.at[n],
            )
        )
    for copy in copies:
        copy.start()
    for copy in copies:
        copy.wait()
    for r in range(4):
        for t in range(2):
            ids, values = tiles[t]
            forward_group(ids, values, panel, acc.at[t], target_group(u, v, c, 2, r))
            start = ((r % 2) * 2 + t) * ROWS
            (low, high)[r // 2][start:start + ROWS, :] = acc[t].astype(BF)


def near_kernel(*refs):
    tiles = (refs[0:2], refs[2:4])
    panel = refs[4]
    outs = {1: refs[5:7], 3: refs[7:9], 0: refs[9:11]}
    acc = refs[11]
    u, v, y, c = coords()
    for p, halves in outs.items():
        for r in range(4):
            for t in range(2):
                ids, values = tiles[t]
                forward_group(ids, values, panel, acc.at[t], target_group(u, v, c, p, r))
                start = ((r % 2) * 2 + t) * ROWS
                halves[r // 2][start:start + ROWS, :] = acc[t].astype(BF)


def relay_kernel(own1, own3, extra1, extra3, out1, out3):
    out1[...] = (own1[...].astype(F32) + extra1[...].astype(F32)).astype(BF)
    out3[...] = (own3[...].astype(F32) + extra3[...].astype(F32)).astype(BF)


def stage_kernel(*refs):
    for n, out in enumerate(refs[6:]):
        here = pl.ds((n % 2) * 2 * ROWS, 2 * ROWS)
        p0, p1, p3 = (
            part[here, :].astype(F32) for part in refs[3 * (n // 2):3 * (n // 2) + 3]
        )
        out[...] = (p0 + (p1 + p3)).astype(BF)


def quad(parts, here):
    p0, p1, p2, p3 = (part[here, :].astype(F32) for part in parts)
    return (p0 + p2) + (p1 + p3)


def finish_kernel(*refs):
    refs[4][...] = quad(refs[:4], pl.ds(0, ROWS)).astype(BF)
    refs[5][...] = quad(refs[:4], pl.ds(ROWS, ROWS)).astype(BF)


def finish_call(parts, name):
    return local_call(
        finish_kernel, name, [vmem()] * 4, [shape(ROWS)] * 2, parts, 8,
        flops=8 * ROWS * HALF,
    )


def point_kernel(scale, *refs):
    own, peer, weight, bias, cotangent = refs[:5]
    out_act, keep_g, give_g, keep_w, give_w, whole, grads, full = refs[5:]
    u, v, y, c = coords()
    whole[:, lanes_of(c)] = own[...]
    whole[:, lanes_of(1 - c)] = peer[...]
    aggregated = whole[...]
    pre = jnp.dot(aggregated, weight[...], preferred_element_type=F32) + bias[...]
    gate = jax.nn.sigmoid(pre)
    out_act[...] = (pre * gate).astype(BF)
    grad_pre = (
        cotangent[...].astype(F32) * gate * (1.0 + pre * (1.0 - gate))
    ).astype(BF)
    grads[...] = lax.dot_general(
        grad_pre, weight[...], (((1,), (1,)), ((), ())), preferred_element_type=F32
    ).astype(BF)
    keep_g[...] = grads[:, lanes_of(c)]
    give_g[...] = grads[:, lanes_of(1 - c)]
    full[...] = lax.dot_general(
        aggregated, grad_pre, (((0,), (0,)), ((), ())), preferred_element_type=F32
    ) * scale
    bias_grad = jnp.sum(grad_pre.astype(F32), axis=0, keepdims=True) * scale
    for out, core in ((keep_w, c), (give_w, 1 - c)):
        out[:HALF, :] = full[rows_at(core * HALF, HALF), :]
        out[HALF:, :] = jnp.broadcast_to(bias_grad, (8, F))


def join_kernel(*refs):
    for n in range(4):
        start = (n % 2) * 2 * ROWS
        refs[4 + n // 2][start:start + 2 * ROWS, :] = refs[n][...]


def backward_group(ids, values, acc, part, base, group):
    for k in range(GRP):
        slot = group * GRP + k
        here = rows_at(base + (ids[0, slot] - group * PB) * BLK, BLK)
        there = rows_at(ids[1, slot] * BLK, BLK)
        acc[there, :] += lax.dot_general(
            values[slot], part[here, :], (((0,), (0,)), ((), ())),
            preferred_element_type=F32,
        )


def early_kernel(*refs):
    tiles = (refs[0:2], refs[2:4])
    parts = {0: refs[4:6], 1: refs[6:8], 3: refs[8:10]}
    acc = refs[10]
    u, v, y, c = coords()
    acc[...] = jnp.zeros_like(acc)
    for p, halves in parts.items():
        for r in range(4):
            for t in range(2):
                ids, values = tiles[t]
                group = source_group(u, v, c, p, r)
                base = ((r % 2) * 2 + t) * ROWS
                backward_group(ids, values, acc, halves[r // 2], base, group)


def late_kernel(*refs):
    tiles = (refs[0:2], refs[2:4])
    start = refs[4]
    parts = refs[5:7]
    outs = refs[7:11]
    acc = refs[11]
    u, v, y, c = coords()
    acc[...] = start[...]
    for r in range(4):
        for t in range(2):
            ids, values = tiles[t]
            group = source_group(u, v, c, 2, r)
            base = ((r % 2) * 2 + t) * ROWS
            backward_group(ids, values, acc, parts[r // 2], base, group)
    for d in range(4):
        first = ahead(y, c, d) * 2
        for t, core in ((0, c), (1, 1 - c)):
            outs[d][t * ROWS:(t + 1) * ROWS, :] = acc[
                rows_at((first + core) * ROWS, ROWS), :
            ].astype(BF)


def sum_kernel(s0, s1, s2, s3, after, out):
    out[...] = (s0[...] + s2[...]) + (s1[...] + s3[...])


def last_kernel(own, peer, mine, theirs, x_grad, weight_grad, bias_grad):
    u, v, y, c = coords()
    x_grad[:, lanes_of(c)] = own[...]
    x_grad[:, lanes_of(1 - c)] = peer[...]
    for source, core in ((mine, c), (theirs, 1 - c)):
        weight_grad[rows_at(core * HALF, HALF), :] = source[:HALF, :]

        @pl.when(core == 0)
        def _(source=source):
            bias_grad[...] = source[HALF:HALF + 1, :]


def permute(value, target):
    pairs = []
    for row in range(8):
        for col in range(16):
            y, c = row // 2, row % 2
            x, z = col // 4, col % 4
            u, v = (z, x) if c else (x, z)
            u, v, y, c = target(u, v, y, c)
            x, z = (v, u) if row % 2 else (u, v)
            pairs.append((row * 16 + col, (y * 2 + c) * 16 + x * 4 + z))
    return lax.ppermute(value, ("row", "col"), pairs)


def along_u(value, d):
    return permute(value, lambda u, v, y, c: ((u + d) % 4, v, y, c))


def along_v(value, d):
    return permute(value, lambda u, v, y, c: (u, (v + d) % 4, y, c))


def along_y(value, d):
    return permute(value, lambda u, v, y, c: (u, v, (y + (1 - 2 * c) * d) % 4, c))


def to_peer(value):
    return permute(value, lambda u, v, y, c: (u, v, y, 1 - c))


def with_u(value, d):
    return value + permute(value, lambda u, v, y, c: (u ^ d, v, y, c))


def with_v(value, d):
    return value + permute(value, lambda u, v, y, c: (u, v ^ d, y, c))


def with_y(value, d):
    return value + permute(value, lambda u, v, y, c: (u, v, y ^ d, c))


def spread(value, along):
    others = {d: along(value, d) for d in (2, 1, 3)}
    return [value, others[1], others[2], others[3]]


def exchange(parts, along):
    others = {d: along(parts[d], d) for d in (2, 1, 3)}
    return [parts[0], others[1], others[2], others[3]]


def shards(x_feat, block_values, block_rows, block_cols, weight, bias, cotangent):
    scale = 1.0 / math.sqrt(65536)
    values = block_values.reshape(128, BLK, BLK)
    slab = 2 * 128 * BLK * BLK * HALF

    keep, give = local_call(
        split_kernel, "split", [vmem()], [shape(ROWS), shape(ROWS)], [x_feat], 4,
    )
    got = to_peer(give)
    got, values, rows, cols = lax.optimization_barrier(
        (got, values, block_rows.reshape(1, 128), block_cols.reshape(1, 128))
    )
    (ids,) = local_call(
        ids_kernel, "ids", [vmem()] * 2, [shape(2, 128, jnp.int32)], [rows, cols], 2,
        moved=2048,
    )
    pair = stack_call([keep, got], "pair")
    pieces = spread(pair, along_y)
    peer_values = to_peer(values)
    peer_ids = to_peer(ids)
    values, weight, bias, cotangent = prologue_call(
        [values, weight, bias.reshape(1, F), cotangent]
    )
    pieces[1], values = lax.optimization_barrier((pieces[1], values))
    tiles = [ids, values, peer_ids, peer_values]
    tile_specs = [smem(), vmem(), smem(), vmem()]

    panel, low, high = local_call(
        far_kernel, "forward_far", tile_specs + [hbm()] * 4,
        [shape(8 * ROWS), shape(4 * ROWS), shape(4 * ROWS)], tiles + pieces, 8,
        flops=slab // 2, moved=6 * MIB,
        scratch=[pltpu.VMEM((2, ROWS, HALF), F32), pltpu.SemaphoreType.DMA((8,))],
    )
    extra = [along_u(low, 1), along_u(high, 3)]
    half = shape(4 * ROWS)
    near1, plain1, plain3, near3, home1, home3 = local_call(
        near_kernel, "forward_near", tile_specs + [vmem()], [half] * 6,
        tiles + [panel], 8, flops=3 * slab // 2, moved=10 * MIB,
        scratch=[pltpu.VMEM((2, ROWS, HALF), F32)],
    )
    plain1, plain3 = along_u(plain1, 1), along_u(plain3, 3)
    mixed1, mixed3 = local_call(
        relay_kernel, "relay_sum", [vmem()] * 4, [half] * 2, [near1, near3] + extra, 8,
        flops=8 * ROWS * HALF, moved=3 * MIB,
    )
    sums = local_call(
        stage_kernel, "stage_sum", [vmem()] * 6, [shape(2 * ROWS)] * 4,
        [home1, along_u(mixed1, 1), plain3, home3, plain1, along_u(mixed3, 3)], 8,
        flops=16 * ROWS * HALF, moved=4 * MIB,
    )
    own, other = finish_call(exchange(sums, along_v), "aggregate")
    out_act, keep_g, give_g, keep_w, give_w = local_call(
        lambda *refs: point_kernel(scale, *refs), "pointwise", [vmem()] * 5,
        [shape(ROWS, F), shape(ROWS), shape(ROWS)] + [shape(HALF + 8, F, F32)] * 2,
        [own, to_peer(other), weight, bias, cotangent], 8, flops=6 * ROWS * F * F,
        moved=2 * MIB,
        scratch=[
            pltpu.VMEM((ROWS, F), BF), pltpu.VMEM((ROWS, F), BF), pltpu.VMEM((F, F), F32),
        ],
    )

    got_g = to_peer(give_g)
    piece = to_peer(give_w)
    got_g, piece = lax.optimization_barrier((got_g, piece))
    grads = stack_call([keep_g, got_g], "pair_grads")
    firsts = spread(grads, along_v)
    piece = with_y(keep_w + piece, 1)
    *firsts, piece = lax.optimization_barrier((*firsts, piece))
    join1, join3 = local_call(
        join_kernel, "join", [vmem()] * 4, [half] * 2, firsts, 8,
    )
    left1, right3 = along_u(join1, 1), along_u(join3, 3)
    left3, right1 = along_u(join3, 1), along_u(join1, 3)
    far = [along_u(left1, 1), along_u(right3, 3)]
    piece = with_y(piece, 2)
    left3, piece = lax.optimization_barrier((left3, piece))
    s0, s1, s2, s3 = spread(piece, along_u)
    (start,) = local_call(
        early_kernel, "backward_early", tile_specs + [vmem()] * 6,
        [shape(8 * ROWS, HALF, F32)],
        tiles + [join1, join3, left1, left3, right1, right3], 8,
        flops=3 * slab // 2, moved=10 * MIB,
    )
    outs = local_call(
        late_kernel, "backward_late", tile_specs + [vmem()] * 3, [shape(2 * ROWS)] * 4,
        tiles + [start] + far, 8, flops=slab // 2, moved=6 * MIB,
        scratch=[pltpu.VMEM((8 * ROWS, HALF), F32)],
    )
    (piece,) = local_call(
        sum_kernel, "sum_u", [vmem()] * 4 + [hbm()], [shape(HALF + 8, F, F32)],
        [s0, s1, s2, s3, outs[0]], 4,
    )
    lasts = exchange(outs, along_y)
    piece = with_v(with_v(piece, 1), 2)
    *lasts, piece = lax.optimization_barrier((*lasts, piece))
    own, other = finish_call(lasts, "sum_x")
    x_grad, weight_grad, bias_grad = local_call(
        last_kernel, "last", [vmem()] * 4,
        [shape(ROWS, F), shape(F, F, F32), shape(1, F, F32)],
        [own, to_peer(other), piece, to_peer(piece)], 8,
    )
    return (out_act, x_grad, weight_grad, bias_grad.reshape(F))


def solution(mesh):
    placed = (
        P(("row", "col"), None),
        P("row", "col", None, None, None),
        P("row", "col", None),
        P("row", "col", None),
        P(),
        P(),
        P(("row", "col"), None),
    )
    return jax.shard_map(
        shards,
        mesh=mesh,
        in_specs=placed,
        out_specs=(P(("row", "col"), None), P(("row", "col"), None), P(), P()),
        check_vma=False,
    )
```

```python
import math

import jax
import jax.numpy as jnp
from jax import lax
from jax.experimental import pallas as pl
from jax.experimental.pallas import tpu as pltpu
from jax.sharding import PartitionSpec as P

BF = jnp.bfloat16
F32 = jnp.float32
BLK = 128
PB = 4
ROWS = 512
HALF = 128
F = 256
GRP = 8
MIB = 1 << 20


def vmem():
    return pl.BlockSpec(memory_space=pltpu.VMEM)


def smem():
    return pl.BlockSpec(memory_space=pltpu.SMEM)


def hbm():
    return pl.BlockSpec(memory_space=pl.ANY)


def coords():
    row = lax.axis_index("row")
    col = lax.axis_index("col")
    y, c = row // 2, row % 2
    x, z = col // 4, col % 4
    return x + c * (z - x), z + c * (x - z), y, c


def group_at(u, v, c):
    return u * (4 - 3 * c) + v * (1 + 3 * c)


def ahead(y, c, d):
    return (y + 4 + (1 - 2 * c) * d) % 4


def target_group(u, v, c, p, r):
    return group_at((u + p) % 4, (v + r) % 4, c)


def source_group(u, v, c, p, r):
    return group_at((u + 4 - p) % 4, (v + 4 - r) % 4, c)


def local_call(kernel, name, ins, outs, args, limit, flops=0, moved=MIB, scratch=()):
    return pl.pallas_call(
        kernel,
        out_shape=outs,
        in_specs=ins,
        out_specs=[vmem()] * len(outs),
        scratch_shapes=list(scratch),
        compiler_params=pltpu.CompilerParams(vmem_limit_bytes=limit * MIB),
        cost_estimate=pl.CostEstimate(
            flops=flops, bytes_accessed=moved, transcendentals=0
        ),
        name=name,
    )(*args)


def shape(rows, width=HALF, dtype=BF):
    return jax.ShapeDtypeStruct((rows, width), dtype)


def lanes_of(core):
    return pl.ds(pl.multiple_of(core * HALF, HALF), HALF)


def rows_at(start, size):
    return pl.ds(pl.multiple_of(start, size), size)


def split_kernel(x_feat, keep, give):
    u, v, y, c = coords()
    keep[...] = x_feat[:, lanes_of(c)]
    give[...] = x_feat[:, lanes_of(1 - c)]


def ids_kernel(rows, cols, ids):
    ids[0:1, :] = rows[...]
    ids[1:2, :] = cols[...]


def stack_kernel(*refs):
    size = refs[0].shape[0]
    for n, ref in enumerate(refs[:-1]):
        refs[-1][n * size:(n + 1) * size, :] = ref[...]


def stack_call(parts, name):
    size, width = parts[0].shape
    return local_call(
        stack_kernel, name, [vmem()] * len(parts), [shape(size * len(parts), width)],
        parts, 8,
    )[0]


def prologue_kernel(*refs):
    count = (len(refs) - 1) // 2
    sems = refs[-1]
    copies = [
        pltpu.make_async_copy(refs[n], refs[count + n], sems.at[n]) for n in range(count)
    ]
    for copy in copies:
        copy.start()
    for copy in copies:
        copy.wait()


def prologue_call(arrays):
    return local_call(
        prologue_kernel, "prologue", [hbm()] * len(arrays),
        [jax.ShapeDtypeStruct(a.shape, a.dtype) for a in arrays], arrays, 8,
        moved=10 * MIB, scratch=[pltpu.SemaphoreType.DMA((len(arrays),))],
    )


def forward_group(ids, values, panel, acc, group):
    acc[...] = jnp.zeros_like(acc)
    for k in range(GRP):
        slot = group * GRP + k
        here = rows_at((ids[0, slot] - group * PB) * BLK, BLK)
        there = rows_at(ids[1, slot] * BLK, BLK)
        acc[here, :] += jnp.dot(
            values[slot], panel[there, :], preferred_element_type=F32
        )


def far_kernel(*refs):
    tiles = (refs[0:2], refs[2:4])
    pieces = refs[4:8]
    panel, low, high, acc = refs[8:]
    u, v, y, c = coords()
    for d in range(4):
        for t, core in ((0, c), (1, 1 - c)):
            shard = ahead(y, c, -d) * 2 + core
            panel[rows_at(shard * ROWS, ROWS), :] = pieces[d][t * ROWS:(t + 1) * ROWS, :]
    for r in range(4):
        for t in range(2):
            ids, values = tiles[t]
            forward_group(ids, values, panel, acc.at[t], target_group(u, v, c, 2, r))
            start = ((r % 2) * 2 + t) * ROWS
            (low, high)[r // 2][start:start + ROWS, :] = acc[t].astype(BF)


def near_kernel(*refs):
    tiles = (refs[0:2], refs[2:4])
    panel = refs[4]
    outs = {1: refs[5:7], 3: refs[7:9], 0: refs[9:11]}
    acc = refs[11]
    u, v, y, c = coords()
    for p, halves in outs.items():
        for r in range(4):
            for t in range(2):
                ids, values = tiles[t]
                forward_group(ids, values, panel, acc.at[t], target_group(u, v, c, p, r))
                start = ((r % 2) * 2 + t) * ROWS
                halves[r // 2][start:start + ROWS, :] = acc[t].astype(BF)


def relay_kernel(own1, own3, extra1, extra3, out1, out3):
    out1[...] = (own1[...].astype(F32) + extra1[...].astype(F32)).astype(BF)
    out3[...] = (own3[...].astype(F32) + extra3[...].astype(F32)).astype(BF)


def stage_kernel(*refs):
    for n, out in enumerate(refs[6:]):
        here = pl.ds((n % 2) * 2 * ROWS, 2 * ROWS)
        p0, p1, p3 = (
            part[here, :].astype(F32) for part in refs[3 * (n // 2):3 * (n // 2) + 3]
        )
        out[...] = (p0 + (p1 + p3)).astype(BF)


def quad(parts, here):
    p0, p1, p2, p3 = (part[here, :].astype(F32) for part in parts)
    return (p0 + p2) + (p1 + p3)


def finish_kernel(*refs):
    refs[4][...] = quad(refs[:4], pl.ds(0, ROWS)).astype(BF)
    refs[5][...] = quad(refs[:4], pl.ds(ROWS, ROWS)).astype(BF)


def finish_call(parts, name):
    return local_call(
        finish_kernel, name, [vmem()] * 4, [shape(ROWS)] * 2, parts, 8,
        flops=8 * ROWS * HALF,
    )


def point_kernel(scale, *refs):
    own, peer, weight, bias, cotangent = refs[:5]
    out_act, keep_g, give_g, keep_w, give_w, whole, grads, full = refs[5:]
    u, v, y, c = coords()
    whole[:, lanes_of(c)] = own[...]
    whole[:, lanes_of(1 - c)] = peer[...]
    aggregated = whole[...]
    pre = jnp.dot(aggregated, weight[...], preferred_element_type=F32) + bias[...]
    gate = jax.nn.sigmoid(pre)
    out_act[...] = (pre * gate).astype(BF)
    grad_pre = (
        cotangent[...].astype(F32) * gate * (1.0 + pre * (1.0 - gate))
    ).astype(BF)
    grads[...] = lax.dot_general(
        grad_pre, weight[...], (((1,), (1,)), ((), ())), preferred_element_type=F32
    ).astype(BF)
    keep_g[...] = grads[:, lanes_of(c)]
    give_g[...] = grads[:, lanes_of(1 - c)]
    full[...] = lax.dot_general(
        aggregated, grad_pre, (((0,), (0,)), ((), ())), preferred_element_type=F32
    ) * scale
    bias_grad = jnp.sum(grad_pre.astype(F32), axis=0, keepdims=True) * scale
    for out, core in ((keep_w, c), (give_w, 1 - c)):
        out[:HALF, :] = full[rows_at(core * HALF, HALF), :]
        out[HALF:, :] = jnp.broadcast_to(bias_grad, (8, F))


def join_kernel(*refs):
    for n in range(4):
        start = (n % 2) * 2 * ROWS
        refs[4 + n // 2][start:start + 2 * ROWS, :] = refs[n][...]


def backward_group(ids, values, acc, part, base, group):
    for k in range(GRP):
        slot = group * GRP + k
        here = rows_at(base + (ids[0, slot] - group * PB) * BLK, BLK)
        there = rows_at(ids[1, slot] * BLK, BLK)
        acc[there, :] += lax.dot_general(
            values[slot], part[here, :], (((0,), (0,)), ((), ())),
            preferred_element_type=F32,
        )


def early_kernel(*refs):
    tiles = (refs[0:2], refs[2:4])
    parts = {0: refs[4:6], 1: refs[6:8], 3: refs[8:10]}
    acc = refs[10]
    u, v, y, c = coords()
    acc[...] = jnp.zeros_like(acc)
    for p, halves in parts.items():
        for r in range(4):
            for t in range(2):
                ids, values = tiles[t]
                group = source_group(u, v, c, p, r)
                base = ((r % 2) * 2 + t) * ROWS
                backward_group(ids, values, acc, halves[r // 2], base, group)


def late_kernel(*refs):
    tiles = (refs[0:2], refs[2:4])
    start = refs[4]
    parts = refs[5:7]
    outs = refs[7:11]
    acc = refs[11]
    u, v, y, c = coords()
    acc[...] = start[...]
    for r in range(4):
        for t in range(2):
            ids, values = tiles[t]
            group = source_group(u, v, c, 2, r)
            base = ((r % 2) * 2 + t) * ROWS
            backward_group(ids, values, acc, parts[r // 2], base, group)
    for d in range(4):
        first = ahead(y, c, d) * 2
        for t, core in ((0, c), (1, 1 - c)):
            outs[d][t * ROWS:(t + 1) * ROWS, :] = acc[
                rows_at((first + core) * ROWS, ROWS), :
            ].astype(BF)


def sum_kernel(s0, s1, s2, s3, after, out):
    out[...] = (s0[...] + s2[...]) + (s1[...] + s3[...])


def last_kernel(own, peer, mine, theirs, x_grad, weight_grad, bias_grad):
    u, v, y, c = coords()
    x_grad[:, lanes_of(c)] = own[...]
    x_grad[:, lanes_of(1 - c)] = peer[...]
    for source, core in ((mine, c), (theirs, 1 - c)):
        weight_grad[rows_at(core * HALF, HALF), :] = source[:HALF, :]

        @pl.when(core == 0)
        def _(source=source):
            bias_grad[...] = source[HALF:HALF + 1, :]


def permute(value, target):
    pairs = []
    for row in range(8):
        for col in range(16):
            y, c = row // 2, row % 2
            x, z = col // 4, col % 4
            u, v = (z, x) if c else (x, z)
            u, v, y, c = target(u, v, y, c)
            x, z = (v, u) if row % 2 else (u, v)
            pairs.append((row * 16 + col, (y * 2 + c) * 16 + x * 4 + z))
    return lax.ppermute(value, ("row", "col"), pairs)


def along_u(value, d):
    return permute(value, lambda u, v, y, c: ((u + d) % 4, v, y, c))


def along_v(value, d):
    return permute(value, lambda u, v, y, c: (u, (v + d) % 4, y, c))


def along_y(value, d):
    return permute(value, lambda u, v, y, c: (u, v, (y + (1 - 2 * c) * d) % 4, c))


def to_peer(value):
    return permute(value, lambda u, v, y, c: (u, v, y, 1 - c))


def with_u(value, d):
    return value + permute(value, lambda u, v, y, c: (u ^ d, v, y, c))


def with_v(value, d):
    return value + permute(value, lambda u, v, y, c: (u, v ^ d, y, c))


def with_y(value, d):
    return value + permute(value, lambda u, v, y, c: (u, v, y ^ d, c))


def spread(value, along):
    others = {d: along(value, d) for d in (2, 1, 3)}
    return [value, others[1], others[2], others[3]]


def exchange(parts, along):
    others = {d: along(parts[d], d) for d in (2, 1, 3)}
    return [parts[0], others[1], others[2], others[3]]


def shards(x_feat, block_values, block_rows, block_cols, weight, bias, cotangent):
    scale = 1.0 / math.sqrt(65536)
    values = block_values.reshape(128, BLK, BLK)
    slab = 2 * 128 * BLK * BLK * HALF

    keep, give = local_call(
        split_kernel, "split", [vmem()], [shape(ROWS), shape(ROWS)], [x_feat], 4,
    )
    got = to_peer(give)
    got, values, rows, cols = lax.optimization_barrier(
        (got, values, block_rows.reshape(1, 128), block_cols.reshape(1, 128))
    )
    (ids,) = local_call(
        ids_kernel, "ids", [vmem()] * 2, [shape(2, 128, jnp.int32)], [rows, cols], 2,
        moved=2048,
    )
    pair = stack_call([keep, got], "pair")
    pieces = spread(pair, along_y)
    peer_values = to_peer(values)
    peer_ids = to_peer(ids)
    values, weight, bias, cotangent = prologue_call(
        [values, weight, bias.reshape(1, F), cotangent]
    )
    pieces[1], values = lax.optimization_barrier((pieces[1], values))
    tiles = [ids, values, peer_ids, peer_values]
    tile_specs = [smem(), vmem(), smem(), vmem()]

    panel, low, high = local_call(
        far_kernel, "forward_far", tile_specs + [vmem()] * 4,
        [shape(8 * ROWS), shape(4 * ROWS), shape(4 * ROWS)], tiles + pieces, 8,
        flops=slab // 2, moved=6 * MIB,
        scratch=[pltpu.VMEM((2, ROWS, HALF), F32)],
    )
    extra = [along_u(low, 1), along_u(high, 3)]
    half = shape(4 * ROWS)
    near1, plain1, plain3, near3, home1, home3 = local_call(
        near_kernel, "forward_near", tile_specs + [vmem()], [half] * 6,
        tiles + [panel], 8, flops=3 * slab // 2, moved=10 * MIB,
        scratch=[pltpu.VMEM((2, ROWS, HALF), F32)],
    )
    plain1, plain3 = along_u(plain1, 1), along_u(plain3, 3)
    mixed1, mixed3 = local_call(
        relay_kernel, "relay_sum", [vmem()] * 4, [half] * 2, [near1, near3] + extra, 8,
        flops=8 * ROWS * HALF, moved=3 * MIB,
    )
    sums = local_call(
        stage_kernel, "stage_sum", [vmem()] * 6, [shape(2 * ROWS)] * 4,
        [home1, along_u(mixed1, 1), plain3, home3, plain1, along_u(mixed3, 3)], 8,
        flops=16 * ROWS * HALF, moved=4 * MIB,
    )
    own, other = finish_call(exchange(sums, along_v), "aggregate")
    out_act, keep_g, give_g, keep_w, give_w = local_call(
        lambda *refs: point_kernel(scale, *refs), "pointwise", [vmem()] * 5,
        [shape(ROWS, F), shape(ROWS), shape(ROWS)] + [shape(HALF + 8, F, F32)] * 2,
        [own, to_peer(other), weight, bias, cotangent], 8, flops=6 * ROWS * F * F,
        moved=2 * MIB,
        scratch=[
            pltpu.VMEM((ROWS, F), BF), pltpu.VMEM((ROWS, F), BF), pltpu.VMEM((F, F), F32),
        ],
    )

    got_g = to_peer(give_g)
    piece = to_peer(give_w)
    got_g, piece = lax.optimization_barrier((got_g, piece))
    grads = stack_call([keep_g, got_g], "pair_grads")
    firsts = spread(grads, along_v)
    piece = with_y(keep_w + piece, 1)
    *firsts, piece = lax.optimization_barrier((*firsts, piece))
    join1, join3 = local_call(
        join_kernel, "join", [vmem()] * 4, [half] * 2, firsts, 8,
    )
    left1, right3 = along_u(join1, 1), along_u(join3, 3)
    left3, right1 = along_u(join3, 1), along_u(join1, 3)
    piece = with_y(piece, 2)
    left1, piece = lax.optimization_barrier((left1, piece))
    far = [along_u(left1, 1), along_u(right3, 3)]
    s0, s1, s2, s3 = spread(piece, along_u)
    (start,) = local_call(
        early_kernel, "backward_early", tile_specs + [vmem()] * 6,
        [shape(8 * ROWS, HALF, F32)],
        tiles + [join1, join3, left1, left3, right1, right3], 8,
        flops=3 * slab // 2, moved=10 * MIB,
    )
    outs = local_call(
        late_kernel, "backward_late", tile_specs + [vmem()] * 3, [shape(2 * ROWS)] * 4,
        tiles + [start] + far, 8, flops=slab // 2, moved=6 * MIB,
        scratch=[pltpu.VMEM((8 * ROWS, HALF), F32)],
    )
    (piece,) = local_call(
        sum_kernel, "sum_u", [vmem()] * 4 + [hbm()], [shape(HALF + 8, F, F32)],
        [s0, s1, s2, s3, outs[0]], 4,
    )
    lasts = exchange(outs, along_y)
    piece = with_v(with_v(piece, 1), 2)
    *lasts, piece = lax.optimization_barrier((*lasts, piece))
    own, other = finish_call(lasts, "sum_x")
    x_grad, weight_grad, bias_grad = local_call(
        last_kernel, "last", [vmem()] * 4,
        [shape(ROWS, F), shape(F, F, F32), shape(1, F, F32)],
        [own, to_peer(other), piece, to_peer(piece)], 8,
    )
    return (out_act, x_grad, weight_grad, bias_grad.reshape(F))


def solution(mesh):
    placed = (
        P(("row", "col"), None),
        P("row", "col", None, None, None),
        P("row", "col", None),
        P("row", "col", None),
        P(),
        P(),
        P(("row", "col"), None),
    )
    return jax.shard_map(
        shards,
        mesh=mesh,
        in_specs=placed,
        out_specs=(P(("row", "col"), None), P(("row", "col"), None), P(), P()),
        check_vma=False,
    )
```

```python
import math

import jax
import jax.numpy as jnp
from jax import lax
from jax.experimental import pallas as pl
from jax.experimental.pallas import tpu as pltpu
from jax.sharding import PartitionSpec as P

BF = jnp.bfloat16
F32 = jnp.float32
BLK = 128
PB = 4
ROWS = 512
HALF = 128
F = 256
GRP = 8
MIB = 1 << 20


def vmem():
    return pl.BlockSpec(memory_space=pltpu.VMEM)


def smem():
    return pl.BlockSpec(memory_space=pltpu.SMEM)


def hbm():
    return pl.BlockSpec(memory_space=pl.ANY)


def coords():
    row = lax.axis_index("row")
    col = lax.axis_index("col")
    y, c = row // 2, row % 2
    x, z = col // 4, col % 4
    return x + c * (z - x), z + c * (x - z), y, c


def group_at(u, v, c):
    return u * (4 - 3 * c) + v * (1 + 3 * c)


def ahead(y, c, d):
    return (y + 4 + (1 - 2 * c) * d) % 4


def target_group(u, v, c, p, r):
    return group_at((u + p) % 4, (v + r) % 4, c)


def source_group(u, v, c, p, r):
    return group_at((u + 4 - p) % 4, (v + 4 - r) % 4, c)


def local_call(kernel, name, ins, outs, args, limit, flops=0, moved=MIB, scratch=()):
    return pl.pallas_call(
        kernel,
        out_shape=outs,
        in_specs=ins,
        out_specs=[vmem()] * len(outs),
        scratch_shapes=list(scratch),
        compiler_params=pltpu.CompilerParams(vmem_limit_bytes=limit * MIB),
        cost_estimate=pl.CostEstimate(
            flops=flops, bytes_accessed=moved, transcendentals=0
        ),
        name=name,
    )(*args)


def shape(rows, width=HALF, dtype=BF):
    return jax.ShapeDtypeStruct((rows, width), dtype)


def lanes_of(core):
    return pl.ds(pl.multiple_of(core * HALF, HALF), HALF)


def rows_at(start, size):
    return pl.ds(pl.multiple_of(start, size), size)


def split_kernel(x_feat, keep, give):
    u, v, y, c = coords()
    keep[...] = x_feat[:, lanes_of(c)]
    give[...] = x_feat[:, lanes_of(1 - c)]


def ids_kernel(rows, cols, ids):
    ids[0:1, :] = rows[...]
    ids[1:2, :] = cols[...]


def stack_kernel(*refs):
    size = refs[0].shape[0]
    for n, ref in enumerate(refs[:-1]):
        refs[-1][n * size:(n + 1) * size, :] = ref[...]


def stack_call(parts, name):
    size, width = parts[0].shape
    return local_call(
        stack_kernel, name, [vmem()] * len(parts), [shape(size * len(parts), width)],
        parts, 8,
    )[0]


def prologue_kernel(*refs):
    count = (len(refs) - 1) // 2
    sems = refs[-1]
    copies = [
        pltpu.make_async_copy(refs[n], refs[count + n], sems.at[n]) for n in range(count)
    ]
    for copy in copies:
        copy.start()
    for copy in copies:
        copy.wait()


def prologue_call(arrays):
    return local_call(
        prologue_kernel, "prologue", [hbm()] * len(arrays),
        [jax.ShapeDtypeStruct(a.shape, a.dtype) for a in arrays], arrays, 8,
        moved=10 * MIB, scratch=[pltpu.SemaphoreType.DMA((len(arrays),))],
    )


def forward_group(ids, values, panel, acc, group):
    acc[...] = jnp.zeros_like(acc)
    for k in range(GRP):
        slot = group * GRP + k
        here = rows_at((ids[0, slot] - group * PB) * BLK, BLK)
        there = rows_at(ids[1, slot] * BLK, BLK)
        acc[here, :] += jnp.dot(
            values[slot], panel[there, :], preferred_element_type=F32
        )


def far_kernel(*refs):
    tiles = (refs[0:2], refs[2:4])
    pieces = refs[4:8]
    panel, low, high, acc = refs[8:]
    u, v, y, c = coords()
    for d in range(4):
        for t, core in ((0, c), (1, 1 - c)):
            shard = ahead(y, c, -d) * 2 + core
            panel[rows_at(shard * ROWS, ROWS), :] = pieces[d][t * ROWS:(t + 1) * ROWS, :]
    for r in range(4):
        for t in range(2):
            ids, values = tiles[t]
            forward_group(ids, values, panel, acc.at[t], target_group(u, v, c, 2, r))
            start = ((r % 2) * 2 + t) * ROWS
            (low, high)[r // 2][start:start + ROWS, :] = acc[t].astype(BF)


def near_kernel(parts, *refs):
    tiles = (refs[0:2], refs[2:4])
    panel = refs[4]
    outs = refs[5:-1]
    acc = refs[-1]
    u, v, y, c = coords()
    for (p, half), out in zip(parts, outs):
        for r in (2 * half, 2 * half + 1):
            for t in range(2):
                ids, values = tiles[t]
                forward_group(ids, values, panel, acc.at[t], target_group(u, v, c, p, r))
                start = ((r % 2) * 2 + t) * ROWS
                out[start:start + ROWS, :] = acc[t].astype(BF)


def relay_kernel(own1, own3, extra1, extra3, out1, out3):
    out1[...] = (own1[...].astype(F32) + extra1[...].astype(F32)).astype(BF)
    out3[...] = (own3[...].astype(F32) + extra3[...].astype(F32)).astype(BF)


def stage_kernel(*refs):
    for n, out in enumerate(refs[6:]):
        here = pl.ds((n % 2) * 2 * ROWS, 2 * ROWS)
        p0, p1, p3 = (
            part[here, :].astype(F32) for part in refs[3 * (n // 2):3 * (n // 2) + 3]
        )
        out[...] = (p0 + (p1 + p3)).astype(BF)


def quad(parts, here):
    p0, p1, p2, p3 = (part[here, :].astype(F32) for part in parts)
    return (p0 + p2) + (p1 + p3)


def finish_kernel(*refs):
    refs[4][...] = quad(refs[:4], pl.ds(0, ROWS)).astype(BF)
    refs[5][...] = quad(refs[:4], pl.ds(ROWS, ROWS)).astype(BF)


def finish_call(parts, name):
    return local_call(
        finish_kernel, name, [vmem()] * 4, [shape(ROWS)] * 2, parts, 8,
        flops=8 * ROWS * HALF,
    )


def point_kernel(scale, *refs):
    own, peer, weight, bias, cotangent = refs[:5]
    out_act, keep_g, give_g, keep_w, give_w, whole, grads, full = refs[5:]
    u, v, y, c = coords()
    whole[:, lanes_of(c)] = own[...]
    whole[:, lanes_of(1 - c)] = peer[...]
    aggregated = whole[...]
    pre = jnp.dot(aggregated, weight[...], preferred_element_type=F32) + bias[...]
    gate = jax.nn.sigmoid(pre)
    out_act[...] = (pre * gate).astype(BF)
    grad_pre = (
        cotangent[...].astype(F32) * gate * (1.0 + pre * (1.0 - gate))
    ).astype(BF)
    grads[...] = lax.dot_general(
        grad_pre, weight[...], (((1,), (1,)), ((), ())), preferred_element_type=F32
    ).astype(BF)
    keep_g[...] = grads[:, lanes_of(c)]
    give_g[...] = grads[:, lanes_of(1 - c)]
    full[...] = lax.dot_general(
        aggregated, grad_pre, (((0,), (0,)), ((), ())), preferred_element_type=F32
    ) * scale
    bias_grad = jnp.sum(grad_pre.astype(F32), axis=0, keepdims=True) * scale
    for out, core in ((keep_w, c), (give_w, 1 - c)):
        out[:HALF, :] = full[rows_at(core * HALF, HALF), :]
        out[HALF:, :] = jnp.broadcast_to(bias_grad, (8, F))


def join_kernel(*refs):
    for n in range(4):
        start = (n % 2) * 2 * ROWS
        refs[4 + n // 2][start:start + 2 * ROWS, :] = refs[n][...]


def backward_group(ids, values, acc, part, base, group):
    for k in range(GRP):
        slot = group * GRP + k
        here = rows_at(base + (ids[0, slot] - group * PB) * BLK, BLK)
        there = rows_at(ids[1, slot] * BLK, BLK)
        acc[there, :] += lax.dot_general(
            values[slot], part[here, :], (((0,), (0,)), ((), ())),
            preferred_element_type=F32,
        )


def early_kernel(*refs):
    tiles = (refs[0:2], refs[2:4])
    parts = {0: refs[4:6], 1: refs[6:8], 3: refs[8:10]}
    acc = refs[10]
    u, v, y, c = coords()
    acc[...] = jnp.zeros_like(acc)
    for p, halves in parts.items():
        for r in range(4):
            for t in range(2):
                ids, values = tiles[t]
                group = source_group(u, v, c, p, r)
                base = ((r % 2) * 2 + t) * ROWS
                backward_group(ids, values, acc, halves[r // 2], base, group)


def late_kernel(*refs):
    tiles = (refs[0:2], refs[2:4])
    start = refs[4]
    parts = refs[5:7]
    outs = refs[7:11]
    acc = refs[11]
    u, v, y, c = coords()
    acc[...] = start[...]
    for r in range(4):
        for t in range(2):
            ids, values = tiles[t]
            group = source_group(u, v, c, 2, r)
            base = ((r % 2) * 2 + t) * ROWS
            backward_group(ids, values, acc, parts[r // 2], base, group)
    for d in range(4):
        first = ahead(y, c, d) * 2
        for t, core in ((0, c), (1, 1 - c)):
            outs[d][t * ROWS:(t + 1) * ROWS, :] = acc[
                rows_at((first + core) * ROWS, ROWS), :
            ].astype(BF)


def sum_kernel(s0, s1, s2, s3, after, out):
    out[...] = (s0[...] + s2[...]) + (s1[...] + s3[...])


def last_kernel(own, peer, mine, theirs, x_grad, weight_grad, bias_grad):
    u, v, y, c = coords()
    x_grad[:, lanes_of(c)] = own[...]
    x_grad[:, lanes_of(1 - c)] = peer[...]
    for source, core in ((mine, c), (theirs, 1 - c)):
        weight_grad[rows_at(core * HALF, HALF), :] = source[:HALF, :]

        @pl.when(core == 0)
        def _(source=source):
            bias_grad[...] = source[HALF:HALF + 1, :]


def permute(value, target):
    pairs = []
    for row in range(8):
        for col in range(16):
            y, c = row // 2, row % 2
            x, z = col // 4, col % 4
            u, v = (z, x) if c else (x, z)
            u, v, y, c = target(u, v, y, c)
            x, z = (v, u) if row % 2 else (u, v)
            pairs.append((row * 16 + col, (y * 2 + c) * 16 + x * 4 + z))
    return lax.ppermute(value, ("row", "col"), pairs)


def along_u(value, d):
    return permute(value, lambda u, v, y, c: ((u + d) % 4, v, y, c))


def along_v(value, d):
    return permute(value, lambda u, v, y, c: (u, (v + d) % 4, y, c))


def along_y(value, d):
    return permute(value, lambda u, v, y, c: (u, v, (y + (1 - 2 * c) * d) % 4, c))


def to_peer(value):
    return permute(value, lambda u, v, y, c: (u, v, y, 1 - c))


def with_u(value, d):
    return value + permute(value, lambda u, v, y, c: (u ^ d, v, y, c))


def with_v(value, d):
    return value + permute(value, lambda u, v, y, c: (u, v ^ d, y, c))


def with_y(value, d):
    return value + permute(value, lambda u, v, y, c: (u, v, y ^ d, c))


def spread(value, along):
    others = {d: along(value, d) for d in (2, 1, 3)}
    return [value, others[1], others[2], others[3]]


def exchange(parts, along):
    others = {d: along(parts[d], d) for d in (2, 1, 3)}
    return [parts[0], others[1], others[2], others[3]]


def shards(x_feat, block_values, block_rows, block_cols, weight, bias, cotangent):
    scale = 1.0 / math.sqrt(65536)
    values = block_values.reshape(128, BLK, BLK)
    slab = 2 * 128 * BLK * BLK * HALF

    keep, give = local_call(
        split_kernel, "split", [vmem()], [shape(ROWS), shape(ROWS)], [x_feat], 4,
    )
    got = to_peer(give)
    got, values, rows, cols = lax.optimization_barrier(
        (got, values, block_rows.reshape(1, 128), block_cols.reshape(1, 128))
    )
    (ids,) = local_call(
        ids_kernel, "ids", [vmem()] * 2, [shape(2, 128, jnp.int32)], [rows, cols], 2,
        moved=2048,
    )
    pair = stack_call([keep, got], "pair")
    pieces = spread(pair, along_y)
    peer_values = to_peer(values)
    peer_ids = to_peer(ids)
    values, weight, bias, cotangent = prologue_call(
        [values, weight, bias.reshape(1, F), cotangent]
    )
    pieces[1], values = lax.optimization_barrier((pieces[1], values))
    tiles = [ids, values, peer_ids, peer_values]
    tile_specs = [smem(), vmem(), smem(), vmem()]

    panel, low, high = local_call(
        far_kernel, "forward_far", tile_specs + [vmem()] * 4,
        [shape(8 * ROWS), shape(4 * ROWS), shape(4 * ROWS)], tiles + pieces, 8,
        flops=slab // 2, moved=6 * MIB,
        scratch=[pltpu.VMEM((2, ROWS, HALF), F32)],
    )
    extra = [along_u(low, 1), along_u(high, 3)]
    half = shape(4 * ROWS)

    def near_call(parts, name):
        return local_call(
            lambda *refs: near_kernel(parts, *refs), name, tile_specs + [vmem()],
            [half] * len(parts), tiles + [panel], 8, flops=len(parts) * slab // 4,
            moved=(1 + len(parts)) * MIB, scratch=[pltpu.VMEM((2, ROWS, HALF), F32)],
        )

    plain1, plain3 = near_call(((1, 1), (3, 0)), "forward_plain")
    near1, near3, home1, home3 = near_call(
        ((1, 0), (3, 1), (0, 0), (0, 1)), "forward_near"
    )
    plain1, plain3 = along_u(plain1, 1), along_u(plain3, 3)
    mixed1, mixed3 = local_call(
        relay_kernel, "relay_sum", [vmem()] * 4, [half] * 2, [near1, near3] + extra, 8,
        flops=8 * ROWS * HALF, moved=3 * MIB,
    )
    sums = local_call(
        stage_kernel, "stage_sum", [vmem()] * 6, [shape(2 * ROWS)] * 4,
        [home1, along_u(mixed1, 1), plain3, home3, plain1, along_u(mixed3, 3)], 8,
        flops=16 * ROWS * HALF, moved=4 * MIB,
    )
    own, other = finish_call(exchange(sums, along_v), "aggregate")
    out_act, keep_g, give_g, keep_w, give_w = local_call(
        lambda *refs: point_kernel(scale, *refs), "pointwise", [vmem()] * 5,
        [shape(ROWS, F), shape(ROWS), shape(ROWS)] + [shape(HALF + 8, F, F32)] * 2,
        [own, to_peer(other), weight, bias, cotangent], 8, flops=6 * ROWS * F * F,
        moved=2 * MIB,
        scratch=[
            pltpu.VMEM((ROWS, F), BF), pltpu.VMEM((ROWS, F), BF), pltpu.VMEM((F, F), F32),
        ],
    )

    got_g = to_peer(give_g)
    piece = to_peer(give_w)
    got_g, piece = lax.optimization_barrier((got_g, piece))
    grads = stack_call([keep_g, got_g], "pair_grads")
    firsts = spread(grads, along_v)
    piece = with_y(keep_w + piece, 1)
    *firsts, piece = lax.optimization_barrier((*firsts, piece))
    join1, join3 = local_call(
        join_kernel, "join", [vmem()] * 4, [half] * 2, firsts, 8,
    )
    left1, right3 = along_u(join1, 1), along_u(join3, 3)
    left3, right1 = along_u(join3, 1), along_u(join1, 3)
    piece = with_y(piece, 2)
    left1, piece = lax.optimization_barrier((left1, piece))
    far = [along_u(left1, 1), along_u(right3, 3)]
    s0, s1, s2, s3 = spread(piece, along_u)
    (start,) = local_call(
        early_kernel, "backward_early", tile_specs + [vmem()] * 6,
        [shape(8 * ROWS, HALF, F32)],
        tiles + [join1, join3, left1, left3, right1, right3], 8,
        flops=3 * slab // 2, moved=10 * MIB,
    )
    outs = local_call(
        late_kernel, "backward_late", tile_specs + [vmem()] * 3, [shape(2 * ROWS)] * 4,
        tiles + [start] + far, 8, flops=slab // 2, moved=6 * MIB,
        scratch=[pltpu.VMEM((8 * ROWS, HALF), F32)],
    )
    (piece,) = local_call(
        sum_kernel, "sum_u", [vmem()] * 4 + [hbm()], [shape(HALF + 8, F, F32)],
        [s0, s1, s2, s3, outs[0]], 4,
    )
    lasts = exchange(outs, along_y)
    piece = with_v(with_v(piece, 1), 2)
    own, other = finish_call(lasts, "sum_x")
    x_grad, weight_grad, bias_grad = local_call(
        last_kernel, "last", [vmem()] * 4,
        [shape(ROWS, F), shape(F, F, F32), shape(1, F, F32)],
        [own, to_peer(other), piece, to_peer(piece)], 8,
    )
    return (out_act, x_grad, weight_grad, bias_grad.reshape(F))


def solution(mesh):
    placed = (
        P(("row", "col"), None),
        P("row", "col", None, None, None),
        P("row", "col", None),
        P("row", "col", None),
        P(),
        P(),
        P(("row", "col"), None),
    )
    return jax.shard_map(
        shards,
        mesh=mesh,
        in_specs=placed,
        out_specs=(P(("row", "col"), None), P(("row", "col"), None), P(), P()),
        check_vma=False,
    )
```

```python
import math

import jax
import jax.numpy as jnp
from jax import lax
from jax.experimental import pallas as pl
from jax.experimental.pallas import tpu as pltpu
from jax.sharding import PartitionSpec as P

BF = jnp.bfloat16
F32 = jnp.float32
BLK = 128
PB = 4
ROWS = 512
HALF = 128
F = 256
GRP = 8
MIB = 1 << 20


def vmem():
    return pl.BlockSpec(memory_space=pltpu.VMEM)


def smem():
    return pl.BlockSpec(memory_space=pltpu.SMEM)


def hbm():
    return pl.BlockSpec(memory_space=pl.ANY)


def coords():
    row = lax.axis_index("row")
    col = lax.axis_index("col")
    y, c = row // 2, row % 2
    x, z = col // 4, col % 4
    return x + c * (z - x), z + c * (x - z), y, c


def group_at(u, v, c):
    return u * (4 - 3 * c) + v * (1 + 3 * c)


def ahead(y, c, d):
    return (y + 4 + (1 - 2 * c) * d) % 4


def target_group(u, v, c, p, r):
    return group_at((u + p) % 4, (v + r) % 4, c)


def source_group(u, v, c, p, r):
    return group_at((u + 4 - p) % 4, (v + 4 - r) % 4, c)


def local_call(kernel, name, ins, outs, args, limit, flops=0, moved=MIB, scratch=()):
    return pl.pallas_call(
        kernel,
        out_shape=outs,
        in_specs=ins,
        out_specs=[vmem()] * len(outs),
        scratch_shapes=list(scratch),
        compiler_params=pltpu.CompilerParams(vmem_limit_bytes=limit * MIB),
        cost_estimate=pl.CostEstimate(
            flops=flops, bytes_accessed=moved, transcendentals=0
        ),
        name=name,
    )(*args)


def shape(rows, width=HALF, dtype=BF):
    return jax.ShapeDtypeStruct((rows, width), dtype)


def lanes_of(core):
    return pl.ds(pl.multiple_of(core * HALF, HALF), HALF)


def rows_at(start, size):
    return pl.ds(pl.multiple_of(start, size), size)


def split_kernel(x_feat, keep, give):
    u, v, y, c = coords()
    keep[...] = x_feat[:, lanes_of(c)]
    give[...] = x_feat[:, lanes_of(1 - c)]


def ids_kernel(rows, cols, ids):
    ids[0:1, :] = rows[...]
    ids[1:2, :] = cols[...]


def stack_kernel(*refs):
    size = refs[0].shape[0]
    for n, ref in enumerate(refs[:-1]):
        refs[-1][n * size:(n + 1) * size, :] = ref[...]


def stack_call(parts, name):
    size, width = parts[0].shape
    return local_call(
        stack_kernel, name, [vmem()] * len(parts), [shape(size * len(parts), width)],
        parts, 8,
    )[0]


def prologue_kernel(*refs):
    count = (len(refs) - 1) // 2
    sems = refs[-1]
    copies = [
        pltpu.make_async_copy(refs[n], refs[count + n], sems.at[n]) for n in range(count)
    ]
    for copy in copies:
        copy.start()
    for copy in copies:
        copy.wait()


def prologue_call(arrays):
    return local_call(
        prologue_kernel, "prologue", [hbm()] * len(arrays),
        [jax.ShapeDtypeStruct(a.shape, a.dtype) for a in arrays], arrays, 8,
        moved=10 * MIB, scratch=[pltpu.SemaphoreType.DMA((len(arrays),))],
    )


def forward_group(ids, values, panel, acc, group):
    acc[...] = jnp.zeros_like(acc)
    for k in range(GRP):
        slot = group * GRP + k
        here = rows_at((ids[0, slot] - group * PB) * BLK, BLK)
        there = rows_at(ids[1, slot] * BLK, BLK)
        acc[here, :] += jnp.dot(
            values[slot], panel[there, :], preferred_element_type=F32
        )


def far_kernel(*refs):
    tiles = (refs[0:2], refs[2:4])
    pieces = refs[4:8]
    panel, low, high, acc = refs[8:]
    u, v, y, c = coords()
    for d in range(4):
        for t, core in ((0, c), (1, 1 - c)):
            shard = ahead(y, c, -d) * 2 + core
            panel[rows_at(shard * ROWS, ROWS), :] = pieces[d][t * ROWS:(t + 1) * ROWS, :]
    for r in range(4):
        for t in range(2):
            ids, values = tiles[t]
            forward_group(ids, values, panel, acc.at[t], target_group(u, v, c, 2, r))
            start = ((r % 2) * 2 + t) * ROWS
            (low, high)[r // 2][start:start + ROWS, :] = acc[t].astype(BF)


def near_kernel(parts, *refs):
    tiles = (refs[0:2], refs[2:4])
    panel = refs[4]
    outs = refs[5:-1]
    acc = refs[-1]
    u, v, y, c = coords()
    for (p, half), out in zip(parts, outs):
        for r in (2 * half, 2 * half + 1):
            for t in range(2):
                ids, values = tiles[t]
                forward_group(ids, values, panel, acc.at[t], target_group(u, v, c, p, r))
                start = ((r % 2) * 2 + t) * ROWS
                out[start:start + ROWS, :] = acc[t].astype(BF)


def relay_kernel(own1, own3, extra1, extra3, out1, out3):
    out1[...] = (own1[...].astype(F32) + extra1[...].astype(F32)).astype(BF)
    out3[...] = (own3[...].astype(F32) + extra3[...].astype(F32)).astype(BF)


def stage_kernel(*refs):
    for n, out in enumerate(refs[6:]):
        here = pl.ds((n % 2) * 2 * ROWS, 2 * ROWS)
        p0, p1, p3 = (
            part[here, :].astype(F32) for part in refs[3 * (n // 2):3 * (n // 2) + 3]
        )
        out[...] = (p0 + (p1 + p3)).astype(BF)


def quad(parts, here):
    p0, p1, p2, p3 = (part[here, :].astype(F32) for part in parts)
    return (p0 + p2) + (p1 + p3)


def finish_kernel(*refs):
    refs[4][...] = quad(refs[:4], pl.ds(0, ROWS)).astype(BF)
    refs[5][...] = quad(refs[:4], pl.ds(ROWS, ROWS)).astype(BF)


def finish_call(parts, name):
    return local_call(
        finish_kernel, name, [vmem()] * 4, [shape(ROWS)] * 2, parts, 8,
        flops=8 * ROWS * HALF,
    )


def point_kernel(*refs):
    own, peer, weight, bias, cotangent = refs[:5]
    out_act, keep_g, give_g, whole, grad_out, grads = refs[5:]
    u, v, y, c = coords()
    whole[:, lanes_of(c)] = own[...]
    whole[:, lanes_of(1 - c)] = peer[...]
    aggregated = whole[...]
    pre = jnp.dot(aggregated, weight[...], preferred_element_type=F32) + bias[...]
    gate = jax.nn.sigmoid(pre)
    out_act[...] = (pre * gate).astype(BF)
    grad_pre = (
        cotangent[...].astype(F32) * gate * (1.0 + pre * (1.0 - gate))
    ).astype(BF)
    grads[...] = lax.dot_general(
        grad_pre, weight[...], (((1,), (1,)), ((), ())), preferred_element_type=F32
    ).astype(BF)
    keep_g[...] = grads[:, lanes_of(c)]
    give_g[...] = grads[:, lanes_of(1 - c)]
    grad_out[...] = grad_pre


def gradient_kernel(scale, whole, grad_pre, keep_w, give_w, full):
    u, v, y, c = coords()
    full[...] = lax.dot_general(
        whole[...], grad_pre[...], (((0,), (0,)), ((), ())), preferred_element_type=F32
    ) * scale
    bias_grad = jnp.sum(grad_pre[...].astype(F32), axis=0, keepdims=True) * scale
    for out, core in ((keep_w, c), (give_w, 1 - c)):
        out[:HALF, :] = full[rows_at(core * HALF, HALF), :]
        out[HALF:, :] = jnp.broadcast_to(bias_grad, (8, F))


def join_kernel(*refs):
    for n in range(4):
        start = (n % 2) * 2 * ROWS
        refs[4 + n // 2][start:start + 2 * ROWS, :] = refs[n][...]


def backward_group(ids, values, acc, part, base, group):
    for k in range(GRP):
        slot = group * GRP + k
        here = rows_at(base + (ids[0, slot] - group * PB) * BLK, BLK)
        there = rows_at(ids[1, slot] * BLK, BLK)
        acc[there, :] += lax.dot_general(
            values[slot], part[here, :], (((0,), (0,)), ((), ())),
            preferred_element_type=F32,
        )


def early_kernel(*refs):
    tiles = (refs[0:2], refs[2:4])
    parts = {0: refs[4:6], 1: refs[6:8], 3: refs[8:10]}
    acc = refs[10]
    u, v, y, c = coords()
    acc[...] = jnp.zeros_like(acc)
    for p, halves in parts.items():
        for r in range(4):
            for t in range(2):
                ids, values = tiles[t]
                group = source_group(u, v, c, p, r)
                base = ((r % 2) * 2 + t) * ROWS
                backward_group(ids, values, acc, halves[r // 2], base, group)


def late_kernel(*refs):
    tiles = (refs[0:2], refs[2:4])
    start = refs[4]
    parts = refs[5:7]
    outs = refs[7:11]
    acc = refs[11]
    u, v, y, c = coords()
    acc[...] = start[...]
    for r in range(4):
        for t in range(2):
            ids, values = tiles[t]
            group = source_group(u, v, c, 2, r)
            base = ((r % 2) * 2 + t) * ROWS
            backward_group(ids, values, acc, parts[r // 2], base, group)
    for d in range(4):
        first = ahead(y, c, d) * 2
        for t, core in ((0, c), (1, 1 - c)):
            outs[d][t * ROWS:(t + 1) * ROWS, :] = acc[
                rows_at((first + core) * ROWS, ROWS), :
            ].astype(BF)


def sum_kernel(s0, s1, s2, s3, after, out):
    out[...] = (s0[...] + s2[...]) + (s1[...] + s3[...])


def last_kernel(own, peer, mine, theirs, x_grad, weight_grad, bias_grad):
    u, v, y, c = coords()
    x_grad[:, lanes_of(c)] = own[...]
    x_grad[:, lanes_of(1 - c)] = peer[...]
    for source, core in ((mine, c), (theirs, 1 - c)):
        weight_grad[rows_at(core * HALF, HALF), :] = source[:HALF, :]

        @pl.when(core == 0)
        def _(source=source):
            bias_grad[...] = source[HALF:HALF + 1, :]


def permute(value, target):
    pairs = []
    for row in range(8):
        for col in range(16):
            y, c = row // 2, row % 2
            x, z = col // 4, col % 4
            u, v = (z, x) if c else (x, z)
            u, v, y, c = target(u, v, y, c)
            x, z = (v, u) if row % 2 else (u, v)
            pairs.append((row * 16 + col, (y * 2 + c) * 16 + x * 4 + z))
    return lax.ppermute(value, ("row", "col"), pairs)


def along_u(value, d):
    return permute(value, lambda u, v, y, c: ((u + d) % 4, v, y, c))


def along_v(value, d):
    return permute(value, lambda u, v, y, c: (u, (v + d) % 4, y, c))


def along_y(value, d):
    return permute(value, lambda u, v, y, c: (u, v, (y + (1 - 2 * c) * d) % 4, c))


def to_peer(value):
    return permute(value, lambda u, v, y, c: (u, v, y, 1 - c))


def with_u(value, d):
    return value + permute(value, lambda u, v, y, c: (u ^ d, v, y, c))


def with_v(value, d):
    return value + permute(value, lambda u, v, y, c: (u, v ^ d, y, c))


def with_y(value, d):
    return value + permute(value, lambda u, v, y, c: (u, v, y ^ d, c))


def spread(value, along):
    others = {d: along(value, d) for d in (2, 1, 3)}
    return [value, others[1], others[2], others[3]]


def exchange(parts, along):
    others = {d: along(parts[d], d) for d in (2, 1, 3)}
    return [parts[0], others[1], others[2], others[3]]


def shards(x_feat, block_values, block_rows, block_cols, weight, bias, cotangent):
    scale = 1.0 / math.sqrt(65536)
    values = block_values.reshape(128, BLK, BLK)
    slab = 2 * 128 * BLK * BLK * HALF

    keep, give = local_call(
        split_kernel, "split", [vmem()], [shape(ROWS), shape(ROWS)], [x_feat], 4,
    )
    got = to_peer(give)
    got, values, rows, cols = lax.optimization_barrier(
        (got, values, block_rows.reshape(1, 128), block_cols.reshape(1, 128))
    )
    (ids,) = local_call(
        ids_kernel, "ids", [vmem()] * 2, [shape(2, 128, jnp.int32)], [rows, cols], 2,
        moved=2048,
    )
    pair = stack_call([keep, got], "pair")
    pieces = spread(pair, along_y)
    peer_values = to_peer(values)
    peer_ids = to_peer(ids)
    values, weight, bias, cotangent = prologue_call(
        [values, weight, bias.reshape(1, F), cotangent]
    )
    pieces[1], values = lax.optimization_barrier((pieces[1], values))
    tiles = [ids, values, peer_ids, peer_values]
    tile_specs = [smem(), vmem(), smem(), vmem()]

    panel, low, high = local_call(
        far_kernel, "forward_far", tile_specs + [vmem()] * 4,
        [shape(8 * ROWS), shape(4 * ROWS), shape(4 * ROWS)], tiles + pieces, 8,
        flops=slab // 2, moved=6 * MIB,
        scratch=[pltpu.VMEM((2, ROWS, HALF), F32)],
    )
    extra = [along_u(low, 1), along_u(high, 3)]
    half = shape(4 * ROWS)

    def near_call(parts, name):
        return local_call(
            lambda *refs: near_kernel(parts, *refs), name, tile_specs + [vmem()],
            [half] * len(parts), tiles + [panel], 8, flops=len(parts) * slab // 4,
            moved=(1 + len(parts)) * MIB, scratch=[pltpu.VMEM((2, ROWS, HALF), F32)],
        )

    plain1, plain3 = near_call(((1, 1), (3, 0)), "forward_plain")
    near1, near3, home1, home3 = near_call(
        ((1, 0), (3, 1), (0, 0), (0, 1)), "forward_near"
    )
    plain1, plain3 = along_u(plain1, 1), along_u(plain3, 3)
    mixed1, mixed3 = local_call(
        relay_kernel, "relay_sum", [vmem()] * 4, [half] * 2, [near1, near3] + extra, 8,
        flops=8 * ROWS * HALF, moved=3 * MIB,
    )
    sums = local_call(
        stage_kernel, "stage_sum", [vmem()] * 6, [shape(2 * ROWS)] * 4,
        [home1, along_u(mixed1, 1), plain3, home3, plain1, along_u(mixed3, 3)], 8,
        flops=16 * ROWS * HALF, moved=4 * MIB,
    )
    own, other = finish_call(exchange(sums, along_v), "aggregate")
    out_act, keep_g, give_g, whole, grad_pre = local_call(
        point_kernel, "pointwise", [vmem()] * 5,
        [shape(ROWS, F), shape(ROWS), shape(ROWS), shape(ROWS, F), shape(ROWS, F)],
        [own, to_peer(other), weight, bias, cotangent], 8, flops=4 * ROWS * F * F,
        moved=2 * MIB, scratch=[pltpu.VMEM((ROWS, F), BF)],
    )
    got_g = to_peer(give_g)
    keep_w, give_w = local_call(
        lambda *refs: gradient_kernel(scale, *refs), "gradients", [vmem()] * 2,
        [shape(HALF + 8, F, F32)] * 2, [whole, grad_pre], 8, flops=2 * ROWS * F * F,
        scratch=[pltpu.VMEM((F, F), F32)],
    )
    piece = to_peer(give_w)
    grads = stack_call([keep_g, got_g], "pair_grads")
    firsts = spread(grads, along_v)
    piece = with_y(keep_w + piece, 1)
    *firsts, piece = lax.optimization_barrier((*firsts, piece))
    join1, join3 = local_call(
        join_kernel, "join", [vmem()] * 4, [half] * 2, firsts, 8,
    )
    left1, right3 = along_u(join1, 1), along_u(join3, 3)
    left3, right1 = along_u(join3, 1), along_u(join1, 3)
    piece = with_y(piece, 2)
    left1, piece = lax.optimization_barrier((left1, piece))
    far = [along_u(left1, 1), along_u(right3, 3)]
    s0, s1, s2, s3 = spread(piece, along_u)
    (start,) = local_call(
        early_kernel, "backward_early", tile_specs + [vmem()] * 6,
        [shape(8 * ROWS, HALF, F32)],
        tiles + [join1, join3, left1, left3, right1, right3], 8,
        flops=3 * slab // 2, moved=10 * MIB,
    )
    outs = local_call(
        late_kernel, "backward_late", tile_specs + [vmem()] * 3, [shape(2 * ROWS)] * 4,
        tiles + [start] + far, 8, flops=slab // 2, moved=6 * MIB,
        scratch=[pltpu.VMEM((8 * ROWS, HALF), F32)],
    )
    (piece,) = local_call(
        sum_kernel, "sum_u", [vmem()] * 4 + [hbm()], [shape(HALF + 8, F, F32)],
        [s0, s1, s2, s3, outs[0]], 4,
    )
    lasts = exchange(outs, along_y)
    piece = with_v(with_v(piece, 1), 2)
    own, other = finish_call(lasts, "sum_x")
    x_grad, weight_grad, bias_grad = local_call(
        last_kernel, "last", [vmem()] * 4,
        [shape(ROWS, F), shape(F, F, F32), shape(1, F, F32)],
        [own, to_peer(other), piece, to_peer(piece)], 8,
    )
    return (out_act, x_grad, weight_grad, bias_grad.reshape(F))


def solution(mesh):
    placed = (
        P(("row", "col"), None),
        P("row", "col", None, None, None),
        P("row", "col", None),
        P("row", "col", None),
        P(),
        P(),
        P(("row", "col"), None),
    )
    return jax.shard_map(
        shards,
        mesh=mesh,
        in_specs=placed,
        out_specs=(P(("row", "col"), None), P(("row", "col"), None), P(), P()),
        check_vma=False,
    )
```
